32 devices in a mesh: groups: 2 (over x), span: 8 (over z, y), head: 2 (over core).
Axes of the slice: x: 2, y: 2, z: 4, core: 2. Of those that a mesh axis runs over, the one named last changes fastest.
Arguments:
- span_states: bfloat16 [2048, 4096], P(('groups', 'span'), 'head'), parts along dimension 0, may hold values from -1.5 to 1.5
- span_queries: bfloat16 [2048, 2048], P(('groups', 'span'), 'head'), parts along dimension 0, may hold values from -1000 to 1000
- span_memory: bfloat16 [2048, 2, 896], P(('groups', 'span'), None, 'head'), parts along dimension 0, may hold values from -1000 to 1000
- passages: bfloat16 [16384, 896], P(('groups', 'span')), parts along dimension 0, may hold values from -1.5 to 1.5
- neighbours: int32 [32, 2], P(('groups', 'span')), parts along dimension 0, may hold values from 0 to 63, as said below
- enc_query_w: bfloat16 [896, 896], P(None, 'head'), may hold values from -0.1875 to 0.1875
- enc_out_w: bfloat16 [896, 896], P(None, 'head'), may hold values from -0.1875 to 0.1875
- kv_weight: bfloat16 [896, 2, 2048], P(None, None, ('head', 'span')), may hold values from -0.1875 to 0.1875
- out_weight: bfloat16 [2048, 4096], P('head', 'span'), may hold values from -0.125 to 0.125
Outputs:
- mixed_states: bfloat16 [2048, 4096], P(('groups', 'span'), 'head'), parts along dimension 0
The draws below stay inside these ranges and needn't reach their ends.
There are 2 independent parts, one for each index of `groups`. The reference program is written for one: setup_inputs(seed, part) draws one part's arguments, and reference() takes and returns one part's arrays. A program takes and returns all parts, laid end to end along the dimension named above; an argument that names none is the same for every part. Nothing has to cross between parts.
Inputs may be any that keep to these rules, and one draw needn't show every extreme that they name: `neighbours`: passage p belongs to index p // 8 of the span axis. Among the spans of one index of the span axis, all 4 passages listed belong to distinct indices.
All inputs are finite; a program needn't handle non-finite values.
Results may differ from the reference program's by a relative error of at most 0.025.
Values may be sent and summed in bfloat16 or wider, within the bound.
A program may use at most 64 MiB of HBM per device.

```python
import math
import jax
import jax.numpy as jnp
from jax import lax

D = 4096
HEADS = 16
HD = 128
E = 896
EHD = 64
CT = 64
PT = 128
NB = 2
PS_DEV = 8
CH_DEV = 2
SPANS = 16
PASSAGES = 64
N_HEAD = 2


def draw_neighbours(key, part):
    device_count = SPANS // CH_DEV

    def per_device(device_key):
        key_order, key_local = jax.random.split(device_key, 2)
        shuffled = jax.random.permutation(key_order, device_count)
        owners = shuffled[:CH_DEV * NB].reshape(CH_DEV, NB)
        local_ids = jax.random.randint(key_local, (CH_DEV, NB), 0, PS_DEV)
        return (owners * PS_DEV + local_ids).astype(jnp.int32)
    device_keys = jax.random.split(jax.random.fold_in(key, 11), device_count)
    return jax.vmap(per_device)(device_keys).reshape(SPANS, NB)


def draw_span_queries(key, part):
    key_base = jax.random.fold_in(jax.random.fold_in(key, 21), 0)
    shape = (SPANS * CT, HEADS * HD)
    values = jnp.clip(jax.random.normal(key_base, shape, jnp.float32), -6.0, 6.0) * 2.0
    return jnp.clip(values, -1000.0, 1000.0).astype(jnp.bfloat16)


def draw_span_memory(key, part):
    key_base = jax.random.fold_in(jax.random.fold_in(key, 31), 0)
    shape = (SPANS * CT, 2, E)
    values = jnp.clip(jax.random.normal(key_base, shape, jnp.float32), -6.0, 6.0)
    return jnp.clip(values, -1000.0, 1000.0).astype(jnp.bfloat16)


def shard_levels(key, dims, cuts, least, largest):
    factor_of, own = 1.0, jax.random.fold_in(key, 6)
    for dim, parts in cuts:
        steps = jnp.exp(jax.random.uniform(jax.random.fold_in(own, dim), (parts,), jnp.float32, least / len(cuts), largest / len(cuts)))
        factor_of = factor_of * jnp.repeat(steps, dims[dim] // parts).reshape([-1 if axis == dim else 1 for axis in range(len(dims))])
    return factor_of


def normal_values(stream_key, shape, scale, reach, shards=(), held_as=jnp.bfloat16):
    gain = shard_levels(stream_key, shape, shards, -0.22, 0.18) if shards else 1.0
    values = jax.random.normal(stream_key, shape, jnp.float32) * scale * gain
    return jnp.minimum(jnp.maximum(values, -reach), reach).astype(held_as)


def setup_inputs(seed: int = 0, part: int = 0) -> dict:
    splits = jax.random.split(jax.random.key(seed), 10)
    part_splits = jax.random.split(jax.random.fold_in(splits[9], part), 10)
    span_states = normal_values(part_splits[0], (SPANS * CT, D), 0.25, 1.5, ((0, 8), (1, 2)))
    span_queries = draw_span_queries(jax.random.fold_in(jax.random.fold_in(splits[9], part), 71), part)
    span_memory = draw_span_memory(jax.random.fold_in(jax.random.fold_in(splits[9], part), 71), part)
    passages = normal_values(part_splits[3], (PASSAGES * PT, E), 0.25, 1.5, ((0, 8),))
    neighbours = draw_neighbours(jax.random.fold_in(jax.random.fold_in(splits[9], part), 71), part)
    enc_query_w = normal_values(splits[5], (E, E), E ** -0.5, 0.1875, ((1, 2),))
    enc_out_w = normal_values(splits[6], (E, E), E ** -0.5, 0.1875, ((1, 2),))
    kv_weight = normal_values(splits[7], (E, 2, HEADS * HD), E ** -0.5, 0.1875, ((2, 16),))
    out_weight = normal_values(splits[8], (HEADS * HD, D), (HEADS * HD) ** -0.5, 0.125, ((0, 2), (1, 8)))
    return dict(span_states=span_states, span_queries=span_queries, span_memory=span_memory, passages=passages, neighbours=neighbours, enc_query_w=enc_query_w, enc_out_w=enc_out_w, kv_weight=kv_weight, out_weight=out_weight)


def rms_rows(values):
    return values * lax.rsqrt(lax.optimization_barrier(jnp.mean(values * values, axis=-1, keepdims=True)) + 1e-06)

def reference(span_states, span_queries, span_memory, passages, neighbours, enc_query_w, enc_out_w, kv_weight, out_weight):
    blocks = passages.reshape(PASSAGES, PT, E)
    half_width = HEADS * HD // N_HEAD
    kv_flat = kv_weight.reshape(E, 2 * HEADS * HD)

    def one_span(span_items):
        chosen, queries, memory, states = span_items
        copies = blocks[chosen]
        flat_rows = copies.reshape(NB * PT, E).astype(jnp.float32)
        normed = rms_rows(flat_rows).astype(jnp.bfloat16)
        enc_query = jnp.dot(normed, enc_query_w, preferred_element_type=jnp.float32).astype(jnp.bfloat16)
        enc_query = enc_query.reshape(NB * PT, E // EHD, EHD)
        key_rows = memory[:, 0].reshape(CT, E // EHD, EHD)
        value_rows = memory[:, 1].reshape(CT, E // EHD, EHD)
        scores = jnp.einsum('qhd,khd->hqk', enc_query.astype(jnp.float32), key_rows.astype(jnp.float32)) / math.sqrt(EHD)
        weights = jax.nn.softmax(scores, axis=-1).astype(jnp.bfloat16)
        mixed_heads = jnp.einsum('hqk,khd->qhd', weights.astype(jnp.float32), value_rows.astype(jnp.float32))
        mixed_heads = mixed_heads.astype(jnp.bfloat16).reshape(NB * PT, E)
        branch = jnp.dot(mixed_heads, enc_out_w.T, preferred_element_type=jnp.float32)
        encoded = rms_rows(flat_rows + branch).astype(jnp.bfloat16)
        dec_kv = jnp.dot(encoded, kv_flat, preferred_element_type=jnp.float32).astype(jnp.bfloat16)
        dec_kv = dec_kv.reshape(NB * PT, 2, HEADS, HD)
        dec_query = queries.reshape(CT, HEADS, HD)
        dec_scores = jnp.einsum('qhd,khd->hqk', dec_query.astype(jnp.float32), dec_kv[:, 0].astype(jnp.float32)) / math.sqrt(HD)
        dec_weights = jax.nn.softmax(dec_scores, axis=-1).astype(jnp.bfloat16)
        attended = jnp.einsum('hqk,khd->qhd', dec_weights.astype(jnp.float32), dec_kv[:, 1].astype(jnp.float32))
        attended = attended.astype(jnp.bfloat16).reshape(CT, HEADS * HD)
        summed = states.astype(jnp.float32)
        for group_index in range(N_HEAD):
            lower = group_index * half_width
            partial_value = jnp.dot(attended[:, lower:lower + half_width], out_weight[lower:lower + half_width], preferred_element_type=jnp.float32)
            rounded = lax.optimization_barrier(partial_value.astype(jnp.bfloat16))
            summed = summed + rounded.astype(jnp.float32)
        return summed.astype(jnp.bfloat16)
    span_rows = lax.map(one_span, (neighbours, span_queries.reshape(SPANS, CT, HEADS * HD), span_memory.reshape(SPANS, CT, 2, E), span_states.reshape(SPANS, CT, D)))
    return span_rows.reshape(SPANS * CT, D)
```

```python
import functools
import math

import jax
import jax.numpy as jnp
from jax import lax
from jax.experimental import pallas as pl
from jax.experimental.pallas import tpu as pltpu
from jax.sharding import PartitionSpec as P

HD = 128
E = 896
EHD = 64
CT = 64
PT = 128
NB = 2
PS_DEV = 8
MESH = pl.DeviceIdType.MESH


epsilon = 1e-06


def rms_rows(values):
    return values * lax.rsqrt(jnp.mean(values * values, axis=-1, keepdims=True) + epsilon)


def softmax_rows(scores):
    top_score = jnp.max(scores, axis=-1, keepdims=True)
    raised = jnp.exp(scores - top_score)
    return raised / jnp.sum(raised, axis=-1, keepdims=True)


def ring_place(span, n):
    odd = span % 2
    return (1 - odd) * (span // 2) + odd * (n - 1 - span // 2)


def ring_span(place, n):
    back = place // (n // 2)
    return (1 - back) * (2 * place) + back * (2 * (n - 1 - place) + 1)


def remote(src, dst, send_sem, recv_sem, **where):
    return pltpu.make_async_remote_copy(
        src_ref=src, dst_ref=dst, send_sem=send_sem, recv_sem=recv_sem,
        device_id=where, device_id_type=MESH,
    )


class Ring:
    def __init__(self, n, own, out, halves, sems):
        me = lax.axis_index("span")
        self.n, self.own, self.out, self.halves, self.sems = n, own, out, halves, sems
        self.place = ring_place(me, n)
        self.right = ring_span((self.place + 1) % n, n)
        self.left = ring_span((self.place + n - 1) % n, n)
        self.steps = n // 2
        self.copies = []

    def start(self, t):
        n = self.n
        pair = []
        for side, target in ((0, self.right), (1, self.left)):
            place = (self.place + (n - t if side == 0 else t)) % n
            block = ring_span(place, n)
            src = self.own if t == 0 else self.out.at[block]
            dst = self.out.at[block]
            if t == self.steps - 1:
                src, dst = self.halves(src, side), self.halves(dst, side)
            copy = remote(src, dst, self.sems.at[0, side, t], self.sems.at[1, side, t], span=target)
            copy.start()
            pair.append(copy)
        self.copies.append(pair)

    def arrived(self, t):
        for copy in self.copies[t]:
            copy.wait_recv()
        n = self.n
        blocks = [ring_span((self.place + n - t - 1) % n, n), ring_span((self.place + t + 1) % n, n)]
        return blocks[:1] if t == self.steps - 1 else blocks

    def finish(self):
        for pair in self.copies:
            for copy in pair:
                copy.wait_send()


def fetch_kernel(
    n, spans, nb_ref, pas_ref, mem_ref, wq_ref, wo_ref, kv_ref,
    cop_ref, memo_ref, wqo_ref, woo_ref, kvg_ref,
    nbg, nbs, picks, got, swap, local_sem, nb_sem, pas_sem, swap_sem, w_sem, ring_sem,
):
    me = lax.axis_index("span")
    head = lax.axis_index("head")
    other = 1 - head
    barrier = pltpu.get_barrier_semaphore()
    for d in range(1, n):
        pl.semaphore_signal(barrier, inc=1, device_id={"span": (me + d) % n}, device_id_type=MESH)
    pl.semaphore_signal(barrier, inc=1, device_id={"head": other}, device_id_type=MESH)
    pl.semaphore_wait(barrier, n)

    nb_copies = []
    for d in range(1, n):
        copy = remote(nb_ref, nbg.at[me], nb_sem.at[0, d], nb_sem.at[1, d], span=(me + d) % n)
        copy.start()
        nb_copies.append(copy)
    own_nb = pltpu.make_async_copy(nb_ref, nbg.at[me], local_sem.at[0])
    own_nb.start()
    w_copies = [
        remote(src, dst, w_sem.at[0, i], w_sem.at[1, i], head=other)
        for i, (src, dst) in enumerate(((mem_ref, memo_ref), (wq_ref, wqo_ref), (wo_ref, woo_ref)))
    ]
    for copy in w_copies:
        copy.start()
    own_kv = pltpu.make_async_copy(kv_ref, kvg_ref.at[me], local_sem.at[1])
    own_kv.start()
    own_nb.wait()
    for copy in nb_copies:
        copy.wait()
    to_scalar = pltpu.make_async_copy(nbg, nbs, local_sem.at[2])
    to_scalar.start()
    to_scalar.wait()

    def pick(requester):
        index = jnp.int32(0)
        for e in range(spans * NB):
            wanted = nbs[requester, 0, e]
            index = index + jnp.where(wanted // PS_DEV == me, wanted % PS_DEV, 0)
        return pas_ref[index, head]

    pas_copies = []
    picks[1] = pick((me + 1) % n)
    for d in range(1, n):
        if d + 1 < n:
            picks[d + 1] = pick((me + d + 1) % n)
        else:
            got[me] = pick(me)
        copy = remote(picks.at[d], got.at[me], pas_sem.at[0, d], pas_sem.at[1, d], span=(me + d) % n)
        copy.start()
        pas_copies.append(copy)

    ring = Ring(n, kv_ref, kvg_ref, lambda ref, side: ref.at[side], ring_sem)
    ring.start(0)
    for copy in pas_copies:
        copy.wait_recv()
    swaps = []
    for c in range(spans):
        swap[c] = got[nbs[me, 0, c * NB + other] // PS_DEV]
    for c in range(spans):
        cop_ref[c, head] = got[nbs[me, 0, c * NB + head] // PS_DEV]
        copy = remote(swap.at[c], cop_ref.at[c, head], swap_sem.at[0, c], swap_sem.at[1, c], head=other)
        copy.start()
        swaps.append(copy)
    for t in range(ring.steps):
        ring.arrived(t)
        if t + 1 < ring.steps:
            ring.start(t + 1)
    own_kv.wait()
    for copy in swaps + w_copies:
        copy.wait()
    for copy in pas_copies:
        copy.wait_send()
    ring.finish()


def out_kernel(
    n, att_ref, w_ref, states_ref, out_ref,
    gathered, part, crossed, summed, back, ring_sem, cross_sem, send_sem, back_sem, local_sem,
):
    me = lax.axis_index("span")
    head = lax.axis_index("head")
    other = 1 - head
    half = n // 2
    owner_head = me // half
    column = me % half
    rows = att_ref.shape[0]
    half_rows = rows // 2
    width = w_ref.shape[1]
    barrier = pltpu.get_barrier_semaphore()
    for d in range(n):
        for hop in range(2):
            if d or hop:
                pl.semaphore_signal(
                    barrier, inc=1,
                    device_id={"span": (me + d) % n, "head": (head + hop) % 2}, device_id_type=MESH,
                )
    pl.semaphore_wait(barrier, 2 * n - 1)

    ring = Ring(n, att_ref, gathered, lambda ref, side: ref.at[pl.ds(side * half_rows, half_rows)], ring_sem)
    ring.start(0)
    crossings, returns = [], []

    def project(block, rows_ref):
        i = len(crossings)
        value = jnp.dot(rows_ref[...], w_ref[...], preferred_element_type=jnp.float32)
        value = value.astype(jnp.bfloat16)
        part[i, 0] = value[:half_rows]
        part[i, 1] = value[half_rows:]
        copy = remote(part.at[i, other], crossed.at[i], cross_sem.at[0, i], cross_sem.at[1, i], head=other)
        crossings.append((copy, block))

    def send_across():
        crossings[-1][0].start()

    def give_back():
        i = len(returns)
        copy, block = crossings[i]
        copy.wait_recv()
        total = part[i, head].astype(jnp.float32) + crossed[i].astype(jnp.float32)
        summed[i] = total.astype(jnp.bfloat16)
        copy = remote(
            summed.at[i], back.at[column, head], send_sem.at[i], back_sem.at[column, head],
            span=block, head=owner_head,
        )
        if i == 0:
            @pl.when(head != owner_head)
            def _():
                copy.start()

            @pl.when(head == owner_head)
            def _():
                back[column, head] = summed[i]
        else:
            copy.start()
        returns.append(copy)

    project(me, att_ref)
    send_across()
    for t in range(ring.steps):
        blocks = ring.arrived(t)
        if t + 1 < ring.steps:
            ring.start(t + 1)
        for block in blocks:
            project(block, gathered.at[block])
            send_across()
            give_back()
    give_back()

    for j in range(half):
        for source in range(2):
            mine = (head * half + j == me) & (head == source)

            @pl.when(jnp.logical_not(mine))
            def _():
                remote(
                    summed.at[0], back.at[j, source], send_sem.at[0], back_sem.at[j, source], head=other,
                ).wait_recv()

            lanes = pl.ds(j * width, width)
            lines = pl.ds(source * half_rows, half_rows)
            out_ref[lines, lanes] = (
                states_ref[lines, lanes].astype(jnp.float32) + back[j, source].astype(jnp.float32)
            ).astype(jnp.bfloat16)
    ring.finish()
    for copy, _ in crossings:
        copy.wait_send()
    for i, copy in enumerate(returns):
        if i == 0:
            @pl.when(head != owner_head)
            def _():
                copy.wait_send()
        else:
            copy.wait_send()


def vmem_call(kernel, collective_id, out_shape, scratch_shapes, *operands):
    outs = out_shape if isinstance(out_shape, (list, tuple)) else [out_shape]
    specs = [pl.BlockSpec(memory_space=pltpu.VMEM)] * len(outs)
    return pl.pallas_call(
        kernel,
        out_shape=out_shape,
        in_specs=[pl.BlockSpec(memory_space=pltpu.VMEM)] * len(operands),
        out_specs=specs if isinstance(out_shape, (list, tuple)) else specs[0],
        scratch_shapes=scratch_shapes,
        compiler_params=pltpu.CompilerParams(collective_id=collective_id, has_side_effects=True),
    )(*operands)


def encode_branch(copies, memory, query_w, out_w):
    span_count = copies.shape[0]
    head_count = memory.shape[3]
    flat_rows = copies.reshape(-1, E).astype(jnp.float32)
    normed = rms_rows(flat_rows).astype(jnp.bfloat16)
    enc_query = jnp.dot(normed, query_w, preferred_element_type=jnp.float32).astype(jnp.bfloat16)
    enc_query = enc_query.reshape(span_count, PT, head_count, EHD)
    scores = jnp.einsum(
        "cqhd,ckhd->chqk", enc_query, memory[:, :, 0], preferred_element_type=jnp.float32
    ) / math.sqrt(EHD)
    weights = softmax_rows(scores).astype(jnp.bfloat16)
    mixed_heads = jnp.einsum(
        "chqk,ckhd->cqhd", weights, memory[:, :, 1], preferred_element_type=jnp.float32
    )
    mixed_heads = mixed_heads.astype(jnp.bfloat16).reshape(-1, head_count * EHD)
    branch = lax.dot_general(
        mixed_heads, out_w, (((1,), (1,)), ((), ())), preferred_element_type=jnp.float32
    )
    return (flat_rows, branch)


def body(
    span_states,
    span_queries,
    span_memory,
    passages,
    neighbours,
    enc_query_w,
    enc_out_w,
    kv_weight,
    out_weight,
):
    n = lax.axis_size("span")
    span_count = neighbours.shape[0]
    bf16 = jnp.bfloat16
    dma = pltpu.SemaphoreType.DMA
    half_rows = PT // 2
    flat_nb = neighbours.reshape(1, -1)
    nb = jnp.pad(flat_nb, ((0, 7), (0, 128 - flat_nb.shape[1])))
    kv = kv_weight.transpose(1, 0, 2)
    memory_flat = span_memory.reshape(span_memory.shape[0], -1)
    sds = jax.ShapeDtypeStruct
    copies, memory_other, query_other, out_other, kv_all = vmem_call(
        functools.partial(fetch_kernel, n, span_count), 0,
        [
            sds((span_count, 2, half_rows, E), bf16),
            sds(memory_flat.shape, bf16),
            sds(enc_query_w.shape, bf16),
            sds(enc_out_w.shape, bf16),
            sds((n,) + kv.shape, bf16),
        ],
        [
            pltpu.VMEM((n, 8, 128), jnp.int32),
            pltpu.SMEM((n, 8, 128), jnp.int32),
            pltpu.VMEM((n, half_rows, E), bf16),
            pltpu.VMEM((n, half_rows, E), bf16),
            pltpu.VMEM((span_count, half_rows, E), bf16),
            dma((3,)),
            dma((2, n)),
            dma((2, n)),
            dma((2, span_count)),
            dma((2, 3)),
            dma((2, 2, n // 2)),
        ],
        nb, passages.reshape(-1, 2, half_rows, E), memory_flat, enc_query_w, enc_out_w, kv,
    )
    query_full = jnp.concatenate([enc_query_w, query_other], axis=1)
    out_full = jnp.concatenate([enc_out_w, out_other], axis=1)
    memory = jnp.concatenate([span_memory, memory_other.reshape(span_memory.shape)], axis=2)
    memory = memory.reshape(span_count, CT, 2, -1, EHD)
    own_rows, own_branch = encode_branch(copies, memory, query_full, out_full)
    encoded = rms_rows(own_rows + own_branch).astype(bf16)
    all_encoded = lax.all_gather(encoded[None], "head", axis=0, tiled=True)
    flat_encoded = all_encoded.reshape(-1, E)
    dec_kv = jnp.einsum(
        "re,nsec->rsnc", flat_encoded, kv_all, preferred_element_type=jnp.float32
    ).astype(bf16)
    head_count = span_queries.shape[1] // HD
    dec_kv = dec_kv.reshape(NB, span_count, PT, 2, head_count, HD)
    dec_query = span_queries.reshape(span_count, CT, head_count, HD)
    scores = jnp.einsum(
        "cqhd,ncphd->chqnp", dec_query, dec_kv[:, :, :, 0], preferred_element_type=jnp.float32
    ) / math.sqrt(HD)
    scores = scores.reshape(span_count, head_count, CT, NB * PT)
    weights = softmax_rows(scores).astype(bf16).reshape(span_count, head_count, CT, NB, PT)
    attended = jnp.einsum(
        "chqnp,ncphd->cqhd", weights, dec_kv[:, :, :, 1], preferred_element_type=jnp.float32
    )
    attended = attended.astype(bf16).reshape(span_count * CT, head_count * HD)
    rows, width = attended.shape[0], out_weight.shape[1]
    return vmem_call(
        functools.partial(out_kernel, n), 1,
        sds(span_states.shape, bf16),
        [
            pltpu.VMEM((n,) + attended.shape, bf16),
            pltpu.VMEM((n, 2, rows // 2, width), bf16),
            pltpu.VMEM((n, rows // 2, width), bf16),
            pltpu.VMEM((n, rows // 2, width), bf16),
            pltpu.VMEM((n // 2, 2, rows // 2, width), bf16),
            dma((2, 2, n // 2)),
            dma((2, n)),
            dma((n,)),
            dma((n // 2, 2)),
            dma((1,)),
        ],
        attended, out_weight, span_states,
    )


def solution(mesh):
    placed = (
        P(("groups", "span"), "head"),
        P(("groups", "span"), "head"),
        P(("groups", "span"), None, "head"),
        P(("groups", "span"), None),
        P(("groups", "span"), None),
        P(None, "head"),
        P(None, "head"),
        P(None, None, ("head", "span")),
        P("head", "span"),
    )
    return jax.shard_map(
        body, mesh=mesh, in_specs=placed, out_specs=P(("groups", "span"), "head"), check_vma=False
    )
```

```python
import functools
import math

import jax
import jax.numpy as jnp
from jax import lax
from jax.experimental import pallas as pl
from jax.experimental.pallas import tpu as pltpu
from jax.sharding import PartitionSpec as P

HD = 128
E = 896
EHD = 64
CT = 64
PT = 128
NB = 2
PS_DEV = 8
MESH = pl.DeviceIdType.MESH


epsilon = 1e-06


def rms_rows(values):
    return values * lax.rsqrt(jnp.mean(values * values, axis=-1, keepdims=True) + epsilon)


def softmax_rows(scores):
    top_score = jnp.max(scores, axis=-1, keepdims=True)
    raised = jnp.exp(scores - top_score)
    return raised / jnp.sum(raised, axis=-1, keepdims=True)


def ring_place(span, n):
    odd = span % 2
    return (1 - odd) * (span // 2) + odd * (n - 1 - span // 2)


def ring_span(place, n):
    back = place // (n // 2)
    return (1 - back) * (2 * place) + back * (2 * (n - 1 - place) + 1)


def remote(src, dst, send_sem, recv_sem, **where):
    return pltpu.make_async_remote_copy(
        src_ref=src, dst_ref=dst, send_sem=send_sem, recv_sem=recv_sem,
        device_id=where, device_id_type=MESH,
    )


class Ring:
    def __init__(self, n, own, slot, halves, sems):
        me = lax.axis_index("span")
        self.n, self.own, self.slot, self.halves, self.sems = n, own, slot, halves, sems
        self.place = ring_place(me, n)
        self.right = ring_span((self.place + 1) % n, n)
        self.left = ring_span((self.place + n - 1) % n, n)
        self.steps = n // 2
        self.copies = []

    def cut(self, ref, t, side):
        return self.halves(ref, side) if t == self.steps - 1 else ref

    def start(self, t):
        n = self.n
        pair = []
        for side, target in ((0, self.right), (1, self.left)):
            block = ring_span((self.place + (n - t if side == 0 else t)) % n, n)
            src = self.own if t == 0 else self.slot(block)
            copy = remote(
                self.cut(src, t, side), self.cut(self.slot(block), t, side),
                self.sems.at[0, side, t], self.sems.at[1, side, t], span=target,
            )
            copy.start()
            pair.append(copy)
        self.copies.append(pair)

    def arrived(self, t):
        for copy in self.copies[t]:
            copy.wait_recv()
        n = self.n
        return [ring_span((self.place + n - t - 1) % n, n), ring_span((self.place + t + 1) % n, n)]

    def finish(self):
        for pair in self.copies:
            for copy in pair:
                copy.wait_send()


def weigh(scores, mask):
    scores = jnp.where(mask, scores, -jnp.inf)
    raised = jnp.exp(scores - jnp.max(scores, axis=-1, keepdims=True))
    return (raised * (1.0 / jnp.sum(raised, axis=-1, keepdims=True))).astype(jnp.bfloat16)


def same_span(shape, rows_each, lanes_each, spans):
    row = lax.broadcasted_iota(jnp.int32, shape, 0) // rows_each
    lane = (lax.broadcasted_iota(jnp.int32, shape, 1) // lanes_each) % spans
    return row == lane


def dot(a, b, dims=((1,), (0,))):
    return lax.dot_general(a, b, (dims, ((), ())), preferred_element_type=jnp.float32)


def fetch_kernel(
    n, groups, spans, fused, nb_ref, pas_ref, mem_ref, wq_ref, wo_ref, kv_ref, ask_ref, *rest,
):
    if fused:
        att_ref, enc, kvg = rest[:3]
    else:
        enc, kvg = rest[:2]
    (
        nbg, nbs, picks, got, swap, cop, mem, wq, wo, query, mixed,
        local_sem, nb_sem, pas_sem, swap_sem, w_sem, enc_sem, ring_sem, twin_sem,
    ) = rest[3 if fused else 2:]
    me = lax.axis_index("span")
    head = lax.axis_index("head")
    group = lax.axis_index("groups")
    other = 1 - head
    twin = group + 1 - 2 * (group % 2)
    part = group % 2
    half_rows = PT // 2
    half_e = wq_ref.shape[0]
    barrier = pltpu.get_barrier_semaphore()
    for d in range(1, n):
        pl.semaphore_signal(barrier, inc=1, device_id={"span": (me + d) % n}, device_id_type=MESH)
    pl.semaphore_signal(barrier, inc=1, device_id={"head": other}, device_id_type=MESH)
    pl.semaphore_signal(barrier, inc=1, device_id={"groups": twin}, device_id_type=MESH)
    pl.semaphore_wait(barrier, n + 1)

    nb_copies = []
    for d in range(1, n):
        copy = remote(nb_ref, nbg.at[me], nb_sem.at[0, d], nb_sem.at[1, d], span=(me + d) % n)
        copy.start()
        nb_copies.append(copy)
    own_nb = pltpu.make_async_copy(nb_ref, nbg.at[me], local_sem.at[0])
    own_nb.start()
    mine = pl.ds(pl.multiple_of(head * half_e, half_e), half_e)
    w_copies, own_copies = [], []
    for i, (src, dst) in enumerate((
        (mem_ref.at[0], mem.at[0, mine]), (mem_ref.at[1], mem.at[1, mine]), (wq_ref, wq.at[mine]), (wo_ref, wo.at[mine]),
    )):
        w_copies.append(remote(src, dst, w_sem.at[0, i], w_sem.at[1, i], head=other))
        w_copies[-1].start()
        own_copies.append(pltpu.make_async_copy(src, dst, local_sem.at[3 + i]))
        own_copies[-1].start()
    own_copies.append(pltpu.make_async_copy(kv_ref, kvg.at[me], local_sem.at[1]))
    own_copies[-1].start()
    own_nb.wait()
    for copy in nb_copies:
        copy.wait()
    to_scalar = pltpu.make_async_copy(nbg, nbs, local_sem.at[2])
    to_scalar.start()
    to_scalar.wait()

    def pick(requester):
        index = jnp.int32(0)
        for e in range(spans * NB):
            wanted = nbs[requester, 0, e]
            index = index + jnp.where(wanted // PS_DEV == me, wanted % PS_DEV, 0)
        return pas_ref[index, head]

    pas_copies = []
    picks[1] = pick((me + 1) % n)
    for d in range(1, n):
        if d + 1 < n:
            picks[d + 1] = pick((me + d + 1) % n)
        else:
            got[me] = pick(me)
        copy = remote(picks.at[d], got.at[me], pas_sem.at[0, d], pas_sem.at[1, d], span=(me + d) % n)
        copy.start()
        pas_copies.append(copy)

    cut_rows = kv_ref.shape[1] // 2
    ring = Ring(
        n, kv_ref.at[part], lambda block: kvg.at[block, part],
        lambda ref, side: ref.at[pl.ds(side * cut_rows, cut_rows)], ring_sem,
    )
    twins = []

    def pass_on(t):
        blocks = ring.arrived(t)
        if t + 1 < ring.steps:
            ring.start(t + 1)
        for side, block in enumerate(blocks):
            piece = ring.cut(ring.slot(block), t, side)
            copy = remote(piece, piece, twin_sem.at[0, side, t], twin_sem.at[1, side, t], groups=twin)
            copy.start()
            twins.append(copy)
        return blocks

    ring.start(0)
    for copy in pas_copies:
        copy.wait_recv()
    swaps = []
    for c in range(spans):
        swap[c] = got[nbs[me, 0, c * NB + other] // PS_DEV]
    for c in range(spans):
        spot = cop.at[pl.ds(pl.multiple_of(c * PT + head * half_rows, half_rows), half_rows)]
        copy = remote(swap.at[c], spot, swap_sem.at[0, c], swap_sem.at[1, c], head=other)
        copy.start()
        swaps.append(copy)
        spot[...] = got[nbs[me, 0, c * NB + head] // PS_DEV]
    for copy in own_copies:
        copy.wait()
    for copy in w_copies:
        copy.wait()
    for copy in swaps:
        copy.wait()

    rows = cop.shape[0]
    tokens = mem.shape[2]
    width = cop.shape[1]
    values = cop[...].astype(jnp.float32)
    query[...] = dot(rms_rows(values).astype(jnp.bfloat16), wq[...], ((1,), (1,))).astype(jnp.bfloat16)
    mask = same_span((rows, tokens), PT, CT, spans)
    feature = lax.broadcasted_iota(jnp.int32, (2 * EHD, tokens), 0) // EHD
    for j in range(width // (2 * EHD)):
        lines = pl.ds(j * 2 * EHD, 2 * EHD)
        total = None
        for e in range(2):
            keys = jnp.where(feature == e, mem[0, lines], jnp.bfloat16(0))
            vals = jnp.where(feature == e, mem[1, lines], jnp.bfloat16(0))
            scores = dot(query[:, lines], keys) * (1.0 / math.sqrt(EHD))
            term = dot(weigh(scores, mask), vals, ((1,), (1,)))
            total = term if e == 0 else total + term
        mixed[:, lines] = total.astype(jnp.bfloat16)
    arrivals = [pass_on(0)]
    branch = dot(mixed[...], wo[...])
    enc[head] = rms_rows(cop[...].astype(jnp.float32) + branch).astype(jnp.bfloat16)
    enc_copy = remote(enc.at[head], enc.at[head], enc_sem.at[0], enc_sem.at[1], head=other)
    enc_copy.start()
    arrivals.append(pass_on(1))
    enc_copy.wait_recv()

    if fused:
        asks = ask_ref.shape[0]
        dec_mask = same_span((asks, NB * rows), CT, PT, spans)

        def attend(block):
            for m in range(kv_ref.shape[2] // HD):
                flat = enc[...].reshape(NB * rows, width)
                lanes = pl.ds(m * HD, HD)
                keys = dot(flat, kvg[block, 0, :, lanes]).astype(jnp.bfloat16)
                vals = dot(flat, kvg[block, 1, :, lanes]).astype(jnp.bfloat16)
                spot = pl.ds(pl.multiple_of(block * kv_ref.shape[2] + m * HD, HD), HD)
                scores = dot(ask_ref[:, spot], keys, ((1,), (1,))) * (1.0 / math.sqrt(HD))
                att_ref[:, spot] = dot(weigh(scores, dec_mask), vals).astype(jnp.bfloat16)

        attend(me)

    for t in range(ring.steps):
        if t >= len(arrivals):
            arrivals.append(pass_on(t))
        for copy in twins[2 * t:2 * t + 2]:
            copy.wait_recv()
        if t + 1 < ring.steps and t + 1 >= len(arrivals):
            arrivals.append(pass_on(t + 1))
        if fused:
            for block in arrivals[t][:1 if t == ring.steps - 1 else 2]:
                attend(block)
    enc_copy.wait_send()
    for copy in pas_copies + twins:
        copy.wait_send()
    ring.finish()


def out_kernel(
    n, att_ref, w_ref, states_ref, out_ref,
    gathered, part, crossed, summed, back, ring_sem, cross_sem, send_sem, back_sem, local_sem,
):
    me = lax.axis_index("span")
    head = lax.axis_index("head")
    other = 1 - head
    half = n // 2
    owner_head = me // half
    column = me % half
    rows = att_ref.shape[0]
    half_rows = rows // 2
    width = w_ref.shape[1]
    barrier = pltpu.get_barrier_semaphore()
    for d in range(n):
        for hop in range(2):
            if d or hop:
                pl.semaphore_signal(
                    barrier, inc=1,
                    device_id={"span": (me + d) % n, "head": (head + hop) % 2}, device_id_type=MESH,
                )
    pl.semaphore_wait(barrier, 2 * n - 1)

    ring = Ring(
        n, att_ref, lambda block: gathered.at[block],
        lambda ref, side: ref.at[pl.ds(side * half_rows, half_rows)], ring_sem,
    )
    ring.start(0)
    crossings, returns = [], []

    def project(block, rows_ref):
        i = len(crossings)
        value = jnp.dot(rows_ref[...], w_ref[...], preferred_element_type=jnp.float32)
        value = value.astype(jnp.bfloat16)
        part[i, 0] = value[:half_rows]
        part[i, 1] = value[half_rows:]
        copy = remote(part.at[i, other], crossed.at[i], cross_sem.at[0, i], cross_sem.at[1, i], head=other)
        crossings.append((copy, block))

    def send_across():
        crossings[-1][0].start()

    def give_back():
        i = len(returns)
        copy, block = crossings[i]
        copy.wait_recv()
        total = part[i, head].astype(jnp.float32) + crossed[i].astype(jnp.float32)
        summed[i] = total.astype(jnp.bfloat16)
        copy = remote(
            summed.at[i], back.at[column, head], send_sem.at[i], back_sem.at[column, head],
            span=block, head=owner_head,
        )
        if i == 0:
            @pl.when(head != owner_head)
            def _():
                copy.start()

            @pl.when(head == owner_head)
            def _():
                back[column, head] = summed[i]
        else:
            copy.start()
        returns.append(copy)

    project(me, att_ref)
    send_across()
    for t in range(ring.steps):
        blocks = ring.arrived(t)
        if t + 1 < ring.steps:
            ring.start(t + 1)
        for block in blocks[:1 if t == ring.steps - 1 else 2]:
            project(block, gathered.at[block])
            send_across()
            give_back()
    give_back()

    for j in range(half):
        for source in range(2):
            mine = (head * half + j == me) & (head == source)

            @pl.when(jnp.logical_not(mine))
            def _():
                remote(
                    summed.at[0], back.at[j, source], send_sem.at[0], back_sem.at[j, source], head=other,
                ).wait_recv()

            lanes = pl.ds(j * width, width)
            lines = pl.ds(source * half_rows, half_rows)
            out_ref[lines, lanes] = (
                states_ref[lines, lanes].astype(jnp.float32) + back[j, source].astype(jnp.float32)
            ).astype(jnp.bfloat16)
    ring.finish()
    for copy, _ in crossings:
        copy.wait_send()
    for i, copy in enumerate(returns):
        if i == 0:
            @pl.when(head != owner_head)
            def _():
                copy.wait_send()
        else:
            copy.wait_send()


def vmem_call(kernel, collective_id, out_shape, scratch_shapes, *operands):
    outs = out_shape if isinstance(out_shape, (list, tuple)) else [out_shape]
    specs = [pl.BlockSpec(memory_space=pltpu.VMEM)] * len(outs)
    return pl.pallas_call(
        kernel,
        out_shape=out_shape,
        in_specs=[pl.BlockSpec(memory_space=pltpu.VMEM)] * len(operands),
        out_specs=specs if isinstance(out_shape, (list, tuple)) else specs[0],
        scratch_shapes=scratch_shapes,
        compiler_params=pltpu.CompilerParams(collective_id=collective_id, has_side_effects=True),
    )(*operands)


def decode(encoded, kv_all, span_queries, span_count):
    dec_kv = jnp.einsum(
        "re,nsec->rsnc", encoded.reshape(-1, E), kv_all, preferred_element_type=jnp.float32
    ).astype(jnp.bfloat16)
    head_count = span_queries.shape[1] // HD
    dec_kv = dec_kv.reshape(NB, span_count, PT, 2, head_count, HD)
    dec_query = span_queries.reshape(span_count, CT, head_count, HD)
    scores = jnp.einsum(
        "cqhd,ncphd->chqnp", dec_query, dec_kv[:, :, :, 0], preferred_element_type=jnp.float32
    ) / math.sqrt(HD)
    scores = scores.reshape(span_count, head_count, CT, NB * PT)
    weights = softmax_rows(scores).astype(jnp.bfloat16)
    weights = weights.reshape(span_count, head_count, CT, NB, PT)
    attended = jnp.einsum(
        "chqnp,ncphd->cqhd", weights, dec_kv[:, :, :, 1], preferred_element_type=jnp.float32
    )
    return attended.astype(jnp.bfloat16).reshape(span_count * CT, head_count * HD)


def body(
    span_states,
    span_queries,
    span_memory,
    passages,
    neighbours,
    enc_query_w,
    enc_out_w,
    kv_weight,
    out_weight,
):
    n = lax.axis_size("span")
    span_count = neighbours.shape[0]
    bf16 = jnp.bfloat16
    dma = pltpu.SemaphoreType.DMA
    half_rows = PT // 2
    flat_nb = neighbours.reshape(1, -1)
    nb = jnp.pad(flat_nb, ((0, 7), (0, 128 - flat_nb.shape[1])))
    kv = kv_weight.transpose(1, 0, 2)
    memory = span_memory.transpose(1, 2, 0)
    rows, tokens = span_count * PT, span_memory.shape[0]
    sds = jax.ShapeDtypeStruct
    fused = kv.shape[2] % HD == 0
    enc_shape, kv_shape = (NB, rows, E), (n,) + kv.shape
    found = vmem_call(
        functools.partial(fetch_kernel, n, lax.axis_size("groups"), span_count, fused), 0,
        [sds(span_queries.shape, bf16)] if fused else [sds(enc_shape, bf16), sds(kv_shape, bf16)],
        ([pltpu.VMEM(enc_shape, bf16), pltpu.VMEM(kv_shape, bf16)] if fused else []) + [
            pltpu.VMEM((n, 8, 128), jnp.int32),
            pltpu.SMEM((n, 8, 128), jnp.int32),
            pltpu.VMEM((n, half_rows, E), bf16),
            pltpu.VMEM((n, half_rows, E), bf16),
            pltpu.VMEM((span_count, half_rows, E), bf16),
            pltpu.VMEM((rows, E), bf16),
            pltpu.VMEM((2, E, tokens), bf16),
            pltpu.VMEM((E, E), bf16),
            pltpu.VMEM((E, E), bf16),
            pltpu.VMEM((rows, E), bf16),
            pltpu.VMEM((rows, E), bf16),
            dma((7,)),
            dma((2, n)),
            dma((2, n)),
            dma((2, span_count)),
            dma((2, 4)),
            dma((2,)),
            dma((2, 2, n // 2)),
            dma((2, 2, n // 2)),
        ],
        nb, passages.reshape(-1, 2, half_rows, E), memory, enc_query_w.T, enc_out_w.T, kv, span_queries,
    )
    attended = found[0] if fused else decode(found[0], found[1], span_queries, span_count)
    rows, width = tokens, out_weight.shape[1]
    return vmem_call(
        functools.partial(out_kernel, n), 1,
        sds(span_states.shape, bf16),
        [
            pltpu.VMEM((n,) + attended.shape, bf16),
            pltpu.VMEM((n, 2, rows // 2, width), bf16),
            pltpu.VMEM((n, rows // 2, width), bf16),
            pltpu.VMEM((n, rows // 2, width), bf16),
            pltpu.VMEM((n // 2, 2, rows // 2, width), bf16),
            dma((2, 2, n // 2)),
            dma((2, n)),
            dma((n,)),
            dma((n // 2, 2)),
            dma((1,)),
        ],
        attended, out_weight, span_states,
    )


def solution(mesh):
    placed = (
        P(("groups", "span"), "head"),
        P(("groups", "span"), "head"),
        P(("groups", "span"), None, "head"),
        P(("groups", "span"), None),
        P(("groups", "span"), None),
        P(None, "head"),
        P(None, "head"),
        P(None, None, ("head", "span")),
        P("head", "span"),
    )
    return jax.shard_map(
        body, mesh=mesh, in_specs=placed, out_specs=P(("groups", "span"), "head"), check_vma=False
    )
```

```python
import functools
import math

import jax
import jax.numpy as jnp
from jax import lax
from jax.experimental import pallas as pl
from jax.experimental.pallas import tpu as pltpu
from jax.sharding import PartitionSpec as P

HD = 128
E = 896
EHD = 64
CT = 64
PT = 128
NB = 2
PS_DEV = 8
MESH = pl.DeviceIdType.MESH


epsilon = 1e-06


def rms_rows(values):
    return values * lax.rsqrt(jnp.mean(values * values, axis=-1, keepdims=True) + epsilon)


def softmax_rows(scores):
    top_score = jnp.max(scores, axis=-1, keepdims=True)
    raised = jnp.exp(scores - top_score)
    return raised / jnp.sum(raised, axis=-1, keepdims=True)


def ring_place(span, n):
    odd = span % 2
    return (1 - odd) * (span // 2) + odd * (n - 1 - span // 2)


def ring_span(place, n):
    back = place // (n // 2)
    return (1 - back) * (2 * place) + back * (2 * (n - 1 - place) + 1)


def remote(src, dst, send_sem, recv_sem, **where):
    return pltpu.make_async_remote_copy(
        src_ref=src, dst_ref=dst, send_sem=send_sem, recv_sem=recv_sem,
        device_id=where, device_id_type=MESH,
    )


class Ring:
    def __init__(self, n, own, slots, sems):
        me = lax.axis_index("span")
        self.n, self.own, self.slots, self.sems = n, own, slots, sems
        self.place = ring_place(me, n)
        self.targets = (ring_span((self.place + 1) % n, n), ring_span((self.place + n - 1) % n, n))
        self.steps = n // 2
        self.copies = {}

    def travels(self, t, side, k):
        return t < self.steps - 1 or k % 2 == side

    def block(self, t, side):
        n = self.n
        return ring_span((self.place + (n - t if side == 0 else t)) % n, n)

    def send(self, t, side, k):
        dst = self.slots(self.block(t, side))[k]
        copy = remote(
            self.own[k] if t == 0 else dst, dst,
            self.sems.at[0, side, t, k], self.sems.at[1, side, t, k], span=self.targets[side],
        )
        copy.start()
        self.copies[t, side, k] = copy

    def start(self):
        for k in range(len(self.own)):
            for side in range(2):
                if self.travels(0, side, k):
                    self.send(0, side, k)

    def advance(self, t, forward=None):
        for k in range(len(self.own)):
            for side in range(2):
                if self.travels(t, side, k):
                    self.copies[t, side, k].wait_recv()
                    if t + 1 < self.steps and self.travels(t + 1, side, k):
                        self.send(t + 1, side, k)
                    if forward is not None:
                        forward(t, side, k, self.block(t + 1, side))
        return [self.block(t + 1, side) for side in range(1 if t == self.steps - 1 else 2)]

    def finish(self):
        for copy in self.copies.values():
            copy.wait_send()


def weigh(scores, mask):
    scores = jnp.where(mask, scores, -jnp.inf)
    raised = jnp.exp(scores - jnp.max(scores, axis=-1, keepdims=True))
    return (raised * (1.0 / jnp.sum(raised, axis=-1, keepdims=True))).astype(jnp.bfloat16)


def same_span(shape, rows_each, lanes_each, spans):
    row = lax.broadcasted_iota(jnp.int32, shape, 0) // rows_each
    lane = (lax.broadcasted_iota(jnp.int32, shape, 1) // lanes_each) % spans
    return row == lane


def dot(a, b, dims=((1,), (0,))):
    return lax.dot_general(a, b, (dims, ((), ())), preferred_element_type=jnp.float32)


def greet_all(n):
    me = lax.axis_index("span")
    head = lax.axis_index("head")
    barrier = pltpu.get_barrier_semaphore()
    for d in range(n):
        for hop in range(2):
            if d or hop:
                pl.semaphore_signal(
                    barrier, inc=1,
                    device_id={"span": (me + d) % n, "head": (head + hop) % 2}, device_id_type=MESH,
                )
    return barrier, 2 * n - 1


def fetch_kernel(
    n, groups, spans, fused, nb_ref, pas_in, mem_ref, wq_ref, wo_ref, kv_ref, ask_in, w_in, states_in, *rest,
):
    if fused:
        (out_ref, enc, kvg, att_ref, *tail) = rest[:4 + 11]
        scratch = rest[4 + 11:]
    else:
        enc, kvg = rest[:2]
        scratch = rest[2:]
    (
        pas_ref, ask_ref, nb_own, nbg, nbs, picks, got, swap, cop, mem, wq, wo, query, mixed,
        local_sem, nb_sem, pas_sem, swap_sem, w_sem, enc_sem, ring_sem, twin_sem,
    ) = scratch
    me = lax.axis_index("span")
    head = lax.axis_index("head")
    group = lax.axis_index("groups")
    other = 1 - head
    twin = group + 1 - 2 * (group % 2)
    part = group % 2
    half_rows = PT // 2
    half_e = wq_ref.shape[0]
    barrier, greeted = greet_all(n)
    pl.semaphore_signal(barrier, inc=1, device_id={"groups": twin}, device_id_type=MESH)
    loads = [pltpu.make_async_copy(pas_in, pas_ref, local_sem.at[7])]
    if fused:
        loads += [
            pltpu.make_async_copy(ask_in, ask_ref, local_sem.at[8]),
            pltpu.make_async_copy(w_in, tail[0], local_sem.at[9]),
            pltpu.make_async_copy(states_in, tail[1], local_sem.at[10]),
        ]
    for copy in loads:
        copy.start()
    nb_own[...] = jnp.zeros_like(nb_own)
    nb_own[:spans, :NB] = nb_ref[...]
    pl.semaphore_wait(barrier, greeted + 1)

    nb_copies = []
    for d in range(1, n):
        copy = remote(nb_own, nbg.at[me], nb_sem.at[0, d], nb_sem.at[1, d], span=(me + d) % n)
        copy.start()
        nb_copies.append(copy)
    own_nb = pltpu.make_async_copy(nb_own, nbg.at[me], local_sem.at[0])
    own_nb.start()

    depth = kv_ref.shape[1]
    half, extra = depth // 2, depth // 4
    near, far = part, 1 - part

    def pieces(ref):
        return [
            ref.at[near, pl.ds(0, half)], ref.at[near, pl.ds(half, half)],
            ref.at[far, pl.ds(0, extra // 2)], ref.at[far, pl.ds(extra // 2, extra // 2)],
        ]

    ring = Ring(n, pieces(kv_ref), lambda block: pieces(kvg.at[block]), ring_sem)
    twins = [[] for _ in range(ring.steps)]

    def to_twin(t, side, k, block):
        if k < 2:
            lines = pl.ds(extra, half - extra) if k == 0 else pl.ds(half, half)
            piece = kvg.at[block, near, lines]
            copy = remote(piece, piece, twin_sem.at[0, side, t, k], twin_sem.at[1, side, t, k], groups=twin)
            copy.start()
            twins[t].append(copy)

    ring.start()
    mine = pl.ds(pl.multiple_of(head * half_e, half_e), half_e)
    w_copies, own_copies = [], []
    for i, (src, dst) in enumerate((
        (mem_ref.at[0], mem.at[0, mine]), (mem_ref.at[1], mem.at[1, mine]), (wq_ref, wq.at[mine]), (wo_ref, wo.at[mine]),
    )):
        w_copies.append(remote(src, dst, w_sem.at[0, i], w_sem.at[1, i], head=other))
        w_copies[-1].start()
        own_copies.append(pltpu.make_async_copy(src, dst, local_sem.at[3 + i]))
        own_copies[-1].start()
    own_copies.append(pltpu.make_async_copy(kv_ref, kvg.at[me], local_sem.at[1]))
    own_copies[-1].start()
    own_nb.wait()
    loads[0].wait()
    for copy in nb_copies:
        copy.wait()
    to_scalar = pltpu.make_async_copy(nbg, nbs, local_sem.at[2])
    to_scalar.start()
    to_scalar.wait()

    def pick(requester):
        index = jnp.int32(0)
        for e in range(spans * NB):
            wanted = nbs[requester, e // NB, e % NB]
            index = index + jnp.where(wanted // PS_DEV == me, wanted % PS_DEV, 0)
        return pas_ref[index, head]

    pas_copies = []
    picks[1] = pick((me + 1) % n)
    for d in range(1, n):
        if d + 1 < n:
            picks[d + 1] = pick((me + d + 1) % n)
        else:
            got[me] = pick(me)
        copy = remote(picks.at[d], got.at[me], pas_sem.at[0, d], pas_sem.at[1, d], span=(me + d) % n)
        copy.start()
        pas_copies.append(copy)

    arrivals = [ring.advance(0, to_twin)]
    for copy in pas_copies:
        copy.wait_recv()
    swaps = []
    for c in range(spans):
        swap[c] = got[nbs[me, c, other] // PS_DEV]
    for c in range(spans):
        spot = cop.at[pl.ds(pl.multiple_of(c * PT + head * half_rows, half_rows), half_rows)]
        copy = remote(swap.at[c], spot, swap_sem.at[0, c], swap_sem.at[1, c], head=other)
        copy.start()
        swaps.append(copy)
        spot[...] = got[nbs[me, c, head] // PS_DEV]
    for copy in own_copies:
        copy.wait()
    for copy in w_copies:
        copy.wait()
    for copy in swaps:
        copy.wait()

    rows = cop.shape[0]
    tokens = mem.shape[2]
    width = cop.shape[1]
    values = cop[...].astype(jnp.float32)
    query[...] = dot(rms_rows(values).astype(jnp.bfloat16), wq[...], ((1,), (1,))).astype(jnp.bfloat16)
    mask = same_span((rows, tokens), PT, CT, spans)
    feature = lax.broadcasted_iota(jnp.int32, (2 * EHD, tokens), 0) // EHD
    for j in range(width // (2 * EHD)):
        lines = pl.ds(j * 2 * EHD, 2 * EHD)
        total = None
        for e in range(2):
            keys = jnp.where(feature == e, mem[0, lines], jnp.bfloat16(0))
            vals = jnp.where(feature == e, mem[1, lines], jnp.bfloat16(0))
            scores = dot(query[:, lines], keys) * (1.0 / math.sqrt(EHD))
            term = dot(weigh(scores, mask), vals, ((1,), (1,)))
            total = term if e == 0 else total + term
        mixed[:, lines] = total.astype(jnp.bfloat16)
    arrivals.append(ring.advance(1, to_twin))
    branch = dot(mixed[...], wo[...])
    enc[head] = rms_rows(cop[...].astype(jnp.float32) + branch).astype(jnp.bfloat16)
    enc_copy = remote(enc.at[head], enc.at[head], enc_sem.at[0], enc_sem.at[1], head=other)
    enc_copy.start()
    if ring.steps > 2:
        arrivals.append(ring.advance(2, to_twin))
    enc_copy.wait_recv()

    if fused:
        loads[1].wait()
        asks = ask_ref.shape[0]
        dec_mask = same_span((asks, NB * rows), CT, PT, spans)

        def attend(block):
            for m in range(kv_ref.shape[2] // HD):
                flat = enc[...].reshape(NB * rows, width)
                lanes = pl.ds(m * HD, HD)
                keys = dot(flat, kvg[block, 0, :, lanes]).astype(jnp.bfloat16)
                vals = dot(flat, kvg[block, 1, :, lanes]).astype(jnp.bfloat16)
                spot = pl.ds(pl.multiple_of(block * kv_ref.shape[2] + m * HD, HD), HD)
                scores = dot(ask_ref[:, spot], keys, ((1,), (1,))) * (1.0 / math.sqrt(HD))
                att_ref[:, spot] = dot(weigh(scores, dec_mask), vals).astype(jnp.bfloat16)

        attend(me)

    for t in range(ring.steps):
        if t >= len(arrivals):
            arrivals.append(ring.advance(t, to_twin))
        for copy in twins[t]:
            copy.wait_recv()
        if fused:
            for block in arrivals[t]:
                attend(block)
    if fused:
        loads[2].wait()
        loads[3].wait()
        out_stage(n, att_ref, tail[0], tail[1], out_ref, *tail[2:])
    enc_copy.wait_send()
    for copy in pas_copies + [copy for pair in twins for copy in pair]:
        copy.wait_send()
    ring.finish()


def out_kernel(n, *refs):
    barrier, greeted = greet_all(n)
    pl.semaphore_wait(barrier, greeted)
    out_stage(n, *refs)


def out_stage(
    n, att_ref, w_ref, states_ref, out_ref,
    gathered, part, crossed, summed, back, ring_sem, cross_sem, send_sem, back_sem,
):
    me = lax.axis_index("span")
    head = lax.axis_index("head")
    other = 1 - head
    half = n // 2
    owner_head = me // half
    column = me % half
    rows = att_ref.shape[0]
    half_rows = rows // 2
    width = w_ref.shape[1]

    def pieces(ref):
        return [ref.at[pl.ds(k * half_rows, half_rows)] for k in range(2)]

    ring = Ring(n, pieces(att_ref), lambda block: pieces(gathered.at[block]), ring_sem)
    ring.start()
    crossings, returns = [], []

    def project(block, rows_ref):
        i = len(crossings)
        value = jnp.dot(rows_ref[...], w_ref[...], preferred_element_type=jnp.float32)
        value = value.astype(jnp.bfloat16)
        part[i, 0] = value[:half_rows]
        part[i, 1] = value[half_rows:]
        copy = remote(part.at[i, other], crossed.at[i], cross_sem.at[0, i], cross_sem.at[1, i], head=other)
        crossings.append((copy, block))

    def send_across():
        crossings[-1][0].start()

    def give_back():
        i = len(returns)
        copy, block = crossings[i]
        copy.wait_recv()
        total = part[i, head].astype(jnp.float32) + crossed[i].astype(jnp.float32)
        summed[i] = total.astype(jnp.bfloat16)
        copy = remote(
            summed.at[i], back.at[column, head], send_sem.at[i], back_sem.at[column, head],
            span=block, head=owner_head,
        )
        if i == 0:
            @pl.when(head != owner_head)
            def _():
                copy.start()

            @pl.when(head == owner_head)
            def _():
                back[column, head] = summed[i]
        else:
            copy.start()
        returns.append(copy)

    project(me, att_ref)
    send_across()
    for t in range(ring.steps):
        for block in ring.advance(t):
            project(block, gathered.at[block])
            send_across()
            give_back()
    give_back()

    for j in range(half):
        for source in range(2):
            mine = (head * half + j == me) & (head == source)

            @pl.when(jnp.logical_not(mine))
            def _():
                remote(
                    summed.at[0], back.at[j, source], send_sem.at[0], back_sem.at[j, source], head=other,
                ).wait_recv()

            lanes = pl.ds(j * width, width)
            lines = pl.ds(source * half_rows, half_rows)
            out_ref[lines, lanes] = (
                states_ref[lines, lanes].astype(jnp.float32) + back[j, source].astype(jnp.float32)
            ).astype(jnp.bfloat16)
    ring.finish()
    for copy, _ in crossings:
        copy.wait_send()
    for i, copy in enumerate(returns):
        if i == 0:
            @pl.when(head != owner_head)
            def _():
                copy.wait_send()
        else:
            copy.wait_send()


def call(kernel, collective_id, out_shape, scratch_shapes, spaces, *operands):
    return pl.pallas_call(
        kernel,
        out_shape=out_shape,
        in_specs=[pl.BlockSpec(memory_space=space) for space in spaces],
        out_specs=[pl.BlockSpec(memory_space=pltpu.VMEM)] * len(out_shape),
        scratch_shapes=scratch_shapes,
        compiler_params=pltpu.CompilerParams(collective_id=collective_id, has_side_effects=True),
    )(*operands)


def decode(encoded, kv_all, span_queries, span_count):
    dec_kv = jnp.einsum(
        "re,nsec->rsnc", encoded.reshape(-1, E), kv_all, preferred_element_type=jnp.float32
    ).astype(jnp.bfloat16)
    head_count = span_queries.shape[1] // HD
    dec_kv = dec_kv.reshape(NB, span_count, PT, 2, head_count, HD)
    dec_query = span_queries.reshape(span_count, CT, head_count, HD)
    scores = jnp.einsum(
        "cqhd,ncphd->chqnp", dec_query, dec_kv[:, :, :, 0], preferred_element_type=jnp.float32
    ) / math.sqrt(HD)
    scores = scores.reshape(span_count, head_count, CT, NB * PT)
    weights = softmax_rows(scores).astype(jnp.bfloat16)
    weights = weights.reshape(span_count, head_count, CT, NB, PT)
    attended = jnp.einsum(
        "chqnp,ncphd->cqhd", weights, dec_kv[:, :, :, 1], preferred_element_type=jnp.float32
    )
    return attended.astype(jnp.bfloat16).reshape(span_count * CT, head_count * HD)


def body(
    span_states,
    span_queries,
    span_memory,
    passages,
    neighbours,
    enc_query_w,
    enc_out_w,
    kv_weight,
    out_weight,
):
    n = lax.axis_size("span")
    span_count = neighbours.shape[0]
    bf16 = jnp.bfloat16
    dma = pltpu.SemaphoreType.DMA
    half_rows = PT // 2
    kv = kv_weight.transpose(1, 0, 2)
    memory = span_memory.transpose(1, 2, 0)
    rows, tokens = span_count * PT, span_memory.shape[0]
    sds = jax.ShapeDtypeStruct
    fused = kv.shape[2] % HD == 0
    enc_shape, kv_shape = (NB, rows, E), (n,) + kv.shape
    states, width = sds(span_states.shape, bf16), out_weight.shape[1]
    out_scratch = [
        pltpu.VMEM((n,) + span_queries.shape, bf16),
        pltpu.VMEM((n, 2, tokens // 2, width), bf16),
        pltpu.VMEM((n, tokens // 2, width), bf16),
        pltpu.VMEM((n, tokens // 2, width), bf16),
        pltpu.VMEM((n // 2, 2, tokens // 2, width), bf16),
        dma((2, 2, n // 2, 2)),
        dma((2, n)),
        dma((n,)),
        dma((n // 2, 2)),
    ]
    scratch = [
        pltpu.VMEM((passages.shape[0] // PT, 2, half_rows, E), bf16),
        pltpu.VMEM(span_queries.shape if fused else (16, 128), bf16),
        pltpu.VMEM((8, 128), jnp.int32),
        pltpu.VMEM((n, 8, 128), jnp.int32),
        pltpu.SMEM((n, 8, 128), jnp.int32),
        pltpu.VMEM((n, half_rows, E), bf16),
        pltpu.VMEM((n, half_rows, E), bf16),
        pltpu.VMEM((span_count, half_rows, E), bf16),
        pltpu.VMEM((rows, E), bf16),
        pltpu.VMEM((2, E, tokens), bf16),
        pltpu.VMEM((E, E), bf16),
        pltpu.VMEM((E, E), bf16),
        pltpu.VMEM((rows, E), bf16),
        pltpu.VMEM((rows, E), bf16),
        dma((11,)),
        dma((2, n)),
        dma((2, n)),
        dma((2, span_count)),
        dma((2, 4)),
        dma((2,)),
        dma((2, 2, n // 2, 4)),
        dma((2, 2, n // 2, 2)),
    ]
    if fused:
        scratch = [
            pltpu.VMEM(enc_shape, bf16), pltpu.VMEM(kv_shape, bf16), pltpu.VMEM(span_queries.shape, bf16),
            pltpu.VMEM(out_weight.shape, bf16), pltpu.VMEM(span_states.shape, bf16),
        ] + out_scratch + scratch
    found = call(
        functools.partial(fetch_kernel, n, lax.axis_size("groups"), span_count, fused), 0,
        [states] if fused else [sds(enc_shape, bf16), sds(kv_shape, bf16)],
        scratch, [pltpu.VMEM] + [pl.ANY] * 8,
        neighbours, passages.reshape(-1, 2, half_rows, E), memory, enc_query_w.T, enc_out_w.T, kv,
        span_queries, out_weight, span_states,
    )
    if fused:
        return found[0]
    attended = decode(found[0], found[1], span_queries, span_count)
    return call(
        functools.partial(out_kernel, n), 1, [states], out_scratch, [pltpu.VMEM] * 3,
        attended, out_weight, span_states,
    )[0]


def solution(mesh):
    placed = (
        P(("groups", "span"), "head"),
        P(("groups", "span"), "head"),
        P(("groups", "span"), None, "head"),
        P(("groups", "span"), None),
        P(("groups", "span"), None),
        P(None, "head"),
        P(None, "head"),
        P(None, None, ("head", "span")),
        P("head", "span"),
    )
    return jax.shard_map(
        body, mesh=mesh, in_specs=placed, out_specs=P(("groups", "span"), "head"), check_vma=False
    )
```

```python
import functools
import math

import jax
import jax.numpy as jnp
from jax import lax
from jax.experimental import pallas as pl
from jax.experimental.pallas import tpu as pltpu
from jax.sharding import PartitionSpec as P

HD = 128
E = 896
EHD = 64
CT = 64
PT = 128
NB = 2
PS_DEV = 8
MESH = pl.DeviceIdType.MESH


epsilon = 1e-06


def rms_rows(values):
    return values * lax.rsqrt(jnp.mean(values * values, axis=-1, keepdims=True) + epsilon)


def softmax_rows(scores):
    top_score = jnp.max(scores, axis=-1, keepdims=True)
    raised = jnp.exp(scores - top_score)
    return raised / jnp.sum(raised, axis=-1, keepdims=True)


def ring_place(span, n):
    odd = span % 2
    return (1 - odd) * (span // 2) + odd * (n - 1 - span // 2)


def ring_span(place, n):
    back = place // (n // 2)
    return (1 - back) * (2 * place) + back * (2 * (n - 1 - place) + 1)


def remote(src, dst, send_sem, recv_sem, **where):
    return pltpu.make_async_remote_copy(
        src_ref=src, dst_ref=dst, send_sem=send_sem, recv_sem=recv_sem,
        device_id=where, device_id_type=MESH,
    )


class Ring:
    def __init__(self, n, own, slots, sems):
        me = lax.axis_index("span")
        self.n, self.own, self.slots, self.sems = n, own, slots, sems
        self.place = ring_place(me, n)
        self.targets = (ring_span((self.place + 1) % n, n), ring_span((self.place + n - 1) % n, n))
        self.steps = n // 2
        self.copies = {}

    def travels(self, t, side, k):
        return t < self.steps - 1 or k % 2 == side

    def block(self, t, side):
        n = self.n
        return ring_span((self.place + (n - t if side == 0 else t)) % n, n)

    def send(self, t, side, k):
        dst = self.slots(self.block(t, side))[k]
        copy = remote(
            self.own[k] if t == 0 else dst, dst,
            self.sems.at[0, side, t, k], self.sems.at[1, side, t, k], span=self.targets[side],
        )
        copy.start()
        self.copies[t, side, k] = copy

    def start(self):
        for k in range(len(self.own)):
            for side in range(2):
                if self.travels(0, side, k):
                    self.send(0, side, k)

    def advance(self, t, forward=None):
        for k in range(len(self.own)):
            for side in range(2):
                if self.travels(t, side, k):
                    self.copies[t, side, k].wait_recv()
                    if t + 1 < self.steps and self.travels(t + 1, side, k):
                        self.send(t + 1, side, k)
                    if forward is not None:
                        forward(t, side, k, self.block(t + 1, side))
        return [self.block(t + 1, side) for side in range(1 if t == self.steps - 1 else 2)]

    def finish(self):
        for copy in self.copies.values():
            copy.wait_send()


def weigh(scores, mask):
    scores = jnp.where(mask, scores, -jnp.inf)
    raised = jnp.exp(scores - jnp.max(scores, axis=-1, keepdims=True))
    return (raised * (1.0 / jnp.sum(raised, axis=-1, keepdims=True))).astype(jnp.bfloat16)


def same_span(shape, rows_each, lanes_each, spans):
    row = lax.broadcasted_iota(jnp.int32, shape, 0) // rows_each
    lane = (lax.broadcasted_iota(jnp.int32, shape, 1) // lanes_each) % spans
    return row == lane


def dot(a, b, dims=((1,), (0,))):
    return lax.dot_general(a, b, (dims, ((), ())), preferred_element_type=jnp.float32)


def greet_all(n):
    me = lax.axis_index("span")
    head = lax.axis_index("head")
    barrier = pltpu.get_barrier_semaphore()
    for d in range(n):
        for hop in range(2):
            if d or hop:
                pl.semaphore_signal(
                    barrier, inc=1,
                    device_id={"span": (me + d) % n, "head": (head + hop) % 2}, device_id_type=MESH,
                )
    return barrier, 2 * n - 1


def fetch_kernel(
    n, groups, spans, fused, nb_ref, pas_in, mem_ref, wq_ref, wo_ref, kv_ref, ask_in, w_in, states_in, *rest,
):
    if fused:
        (out_ref, enc, kvg, att_ref, *tail) = rest[:4 + 11]
        scratch = rest[4 + 11:]
    else:
        enc, kvg = rest[:2]
        scratch = rest[2:]
    (
        pas_ref, ask_ref, nb_own, nbg, nbs, picks, got, swap, cop, mem, wq, wo, query, mixed,
        local_sem, nb_sem, pas_sem, swap_sem, w_sem, enc_sem, ring_sem, twin_sem,
    ) = scratch
    me = lax.axis_index("span")
    head = lax.axis_index("head")
    group = lax.axis_index("groups")
    other = 1 - head
    twin = group + 1 - 2 * (group % 2)
    part = group % 2
    half_rows = PT // 2
    half_e = wq_ref.shape[0]
    barrier, greeted = greet_all(n)
    pl.semaphore_signal(barrier, inc=1, device_id={"groups": twin}, device_id_type=MESH)
    loads = [pltpu.make_async_copy(pas_in, pas_ref, local_sem.at[7])]
    if fused:
        loads += [
            pltpu.make_async_copy(ask_in, ask_ref, local_sem.at[8]),
            pltpu.make_async_copy(w_in, tail[0], local_sem.at[9]),
            pltpu.make_async_copy(states_in, tail[1], local_sem.at[10]),
        ]
    for copy in loads:
        copy.start()
    nb_own[...] = jnp.zeros_like(nb_own)
    nb_own[:spans, :NB] = nb_ref[...]
    pl.semaphore_wait(barrier, greeted + 1)

    nb_copies = []
    for d in range(1, n):
        copy = remote(nb_own, nbg.at[me], nb_sem.at[0, d], nb_sem.at[1, d], span=(me + d) % n)
        copy.start()
        nb_copies.append(copy)
    own_nb = pltpu.make_async_copy(nb_own, nbg.at[me], local_sem.at[0])
    own_nb.start()

    depth = kv_ref.shape[1]
    half, extra = depth // 2, depth // 28 * 3
    near, far = part, 1 - part

    def pieces(ref):
        return [
            ref.at[near, pl.ds(0, half)], ref.at[near, pl.ds(half, half)],
            ref.at[far, pl.ds(0, extra // 2)], ref.at[far, pl.ds(extra // 2, extra // 2)],
        ]

    ring = Ring(n, pieces(kv_ref), lambda block: pieces(kvg.at[block]), ring_sem)
    twins = [[] for _ in range(ring.steps)]

    def to_twin(t, side, k, block):
        if k < 2:
            lines = pl.ds(extra, half - extra) if k == 0 else pl.ds(half, half)
            piece = kvg.at[block, near, lines]
            copy = remote(piece, piece, twin_sem.at[0, side, t, k], twin_sem.at[1, side, t, k], groups=twin)
            copy.start()
            twins[t].append(copy)

    ring.start()
    mine = pl.ds(pl.multiple_of(head * half_e, half_e), half_e)
    w_copies, own_copies = [], []
    for i, (src, dst) in enumerate((
        (mem_ref.at[0], mem.at[0, mine]), (mem_ref.at[1], mem.at[1, mine]), (wq_ref, wq.at[mine]), (wo_ref, wo.at[mine]),
    )):
        w_copies.append(remote(src, dst, w_sem.at[0, i], w_sem.at[1, i], head=other))
        w_copies[-1].start()
        own_copies.append(pltpu.make_async_copy(src, dst, local_sem.at[3 + i]))
        own_copies[-1].start()
    own_copies.append(pltpu.make_async_copy(kv_ref, kvg.at[me], local_sem.at[1]))
    own_copies[-1].start()
    own_nb.wait()
    loads[0].wait()
    for copy in nb_copies:
        copy.wait()
    to_scalar = pltpu.make_async_copy(nbg, nbs, local_sem.at[2])
    to_scalar.start()
    to_scalar.wait()

    def pick(requester):
        index = jnp.int32(0)
        for e in range(spans * NB):
            wanted = nbs[requester, e // NB, e % NB]
            index = index + jnp.where(wanted // PS_DEV == me, wanted % PS_DEV, 0)
        return pas_ref[index, head]

    pas_copies = []
    picks[1] = pick((me + 1) % n)
    for d in range(1, n):
        if d + 1 < n:
            picks[d + 1] = pick((me + d + 1) % n)
        else:
            got[me] = pick(me)
        copy = remote(picks.at[d], got.at[me], pas_sem.at[0, d], pas_sem.at[1, d], span=(me + d) % n)
        copy.start()
        pas_copies.append(copy)

    arrivals = [ring.advance(0, to_twin)]
    for copy in pas_copies:
        copy.wait_recv()
    swaps = []
    for c in range(spans):
        swap[c] = got[nbs[me, c, other] // PS_DEV]
    for c in range(spans):
        spot = cop.at[pl.ds(pl.multiple_of(c * PT + head * half_rows, half_rows), half_rows)]
        copy = remote(swap.at[c], spot, swap_sem.at[0, c], swap_sem.at[1, c], head=other)
        copy.start()
        swaps.append(copy)
        spot[...] = got[nbs[me, c, head] // PS_DEV]
    for copy in own_copies:
        copy.wait()
    for copy in w_copies:
        copy.wait()
    for copy in swaps:
        copy.wait()

    arrivals.append(ring.advance(1, to_twin))
    rows = cop.shape[0]
    tokens = mem.shape[2]
    width = cop.shape[1]
    values = cop[...].astype(jnp.float32)
    query[...] = dot(rms_rows(values).astype(jnp.bfloat16), wq[...], ((1,), (1,))).astype(jnp.bfloat16)
    mask = same_span((rows, tokens), PT, CT, spans)
    feature = lax.broadcasted_iota(jnp.int32, (2 * EHD, tokens), 0) // EHD
    for j in range(width // (2 * EHD)):
        lines = pl.ds(j * 2 * EHD, 2 * EHD)
        total = None
        for e in range(2):
            keys = jnp.where(feature == e, mem[0, lines], jnp.bfloat16(0))
            vals = jnp.where(feature == e, mem[1, lines], jnp.bfloat16(0))
            scores = dot(query[:, lines], keys) * (1.0 / math.sqrt(EHD))
            term = dot(weigh(scores, mask), vals, ((1,), (1,)))
            total = term if e == 0 else total + term
        mixed[:, lines] = total.astype(jnp.bfloat16)
    branch = dot(mixed[...], wo[...])
    enc[head] = rms_rows(cop[...].astype(jnp.float32) + branch).astype(jnp.bfloat16)
    enc_copy = remote(enc.at[head], enc.at[head], enc_sem.at[0], enc_sem.at[1], head=other)
    enc_copy.start()
    if ring.steps > 2:
        arrivals.append(ring.advance(2, to_twin))
    enc_copy.wait_recv()

    if fused:
        loads[1].wait()
        asks = ask_ref.shape[0]
        dec_mask = same_span((asks, NB * rows), CT, PT, spans)

        def attend(block):
            for m in range(kv_ref.shape[2] // HD):
                flat = enc[...].reshape(NB * rows, width)
                lanes = pl.ds(m * HD, HD)
                keys = dot(flat, kvg[block, 0, :, lanes]).astype(jnp.bfloat16)
                vals = dot(flat, kvg[block, 1, :, lanes]).astype(jnp.bfloat16)
                spot = pl.ds(pl.multiple_of(block * kv_ref.shape[2] + m * HD, HD), HD)
                scores = dot(ask_ref[:, spot], keys, ((1,), (1,))) * (1.0 / math.sqrt(HD))
                att_ref[:, spot] = dot(weigh(scores, dec_mask), vals).astype(jnp.bfloat16)

        attend(me)

    for t in range(ring.steps):
        if t >= len(arrivals):
            arrivals.append(ring.advance(t, to_twin))
        for copy in twins[t]:
            copy.wait_recv()
        if fused:
            for block in arrivals[t]:
                attend(block)
    if fused:
        loads[2].wait()
        loads[3].wait()
        out_stage(n, att_ref, tail[0], tail[1], out_ref, *tail[2:])
    enc_copy.wait_send()
    for copy in pas_copies + [copy for pair in twins for copy in pair]:
        copy.wait_send()
    ring.finish()


def out_kernel(n, *refs):
    barrier, greeted = greet_all(n)
    pl.semaphore_wait(barrier, greeted)
    out_stage(n, *refs)


def out_stage(
    n, att_ref, w_ref, states_ref, out_ref,
    gathered, part, crossed, summed, back, ring_sem, cross_sem, send_sem, back_sem,
):
    me = lax.axis_index("span")
    head = lax.axis_index("head")
    other = 1 - head
    half = n // 2
    owner_head = me // half
    column = me % half
    rows = att_ref.shape[0]
    half_rows = rows // 2
    width = w_ref.shape[1]

    def pieces(ref):
        return [ref.at[pl.ds(k * half_rows, half_rows)] for k in range(2)]

    ring = Ring(n, pieces(att_ref), lambda block: pieces(gathered.at[block]), ring_sem)
    ring.start()
    crossings, returns = [], []

    def project(block, rows_ref):
        i = len(crossings)
        value = jnp.dot(rows_ref[...], w_ref[...], preferred_element_type=jnp.float32)
        value = value.astype(jnp.bfloat16)
        part[i, 0] = value[:half_rows]
        part[i, 1] = value[half_rows:]
        copy = remote(part.at[i, other], crossed.at[i], cross_sem.at[0, i], cross_sem.at[1, i], head=other)
        crossings.append((copy, block))

    def send_across():
        crossings[-1][0].start()

    def give_back():
        i = len(returns)
        copy, block = crossings[i]
        copy.wait_recv()
        total = part[i, head].astype(jnp.float32) + crossed[i].astype(jnp.float32)
        summed[i] = total.astype(jnp.bfloat16)
        copy = remote(
            summed.at[i], back.at[column, head], send_sem.at[i], back_sem.at[column, head],
            span=block, head=owner_head,
        )
        if i == 0:
            @pl.when(head != owner_head)
            def _():
                copy.start()

            @pl.when(head == owner_head)
            def _():
                back[column, head] = summed[i]
        else:
            copy.start()
        returns.append(copy)

    project(me, att_ref)
    send_across()
    for t in range(ring.steps):
        for block in ring.advance(t):
            project(block, gathered.at[block])
            send_across()
            give_back()
    give_back()

    for j in range(half):
        for source in range(2):
            mine = (head * half + j == me) & (head == source)

            @pl.when(jnp.logical_not(mine))
            def _():
                remote(
                    summed.at[0], back.at[j, source], send_sem.at[0], back_sem.at[j, source], head=other,
                ).wait_recv()

            lanes = pl.ds(j * width, width)
            lines = pl.ds(source * half_rows, half_rows)
            out_ref[lines, lanes] = (
                states_ref[lines, lanes].astype(jnp.float32) + back[j, source].astype(jnp.float32)
            ).astype(jnp.bfloat16)
    ring.finish()
    for copy, _ in crossings:
        copy.wait_send()
    for i, copy in enumerate(returns):
        if i == 0:
            @pl.when(head != owner_head)
            def _():
                copy.wait_send()
        else:
            copy.wait_send()


def call(kernel, collective_id, out_shape, scratch_shapes, spaces, *operands):
    return pl.pallas_call(
        kernel,
        out_shape=out_shape,
        in_specs=[pl.BlockSpec(memory_space=space) for space in spaces],
        out_specs=[pl.BlockSpec(memory_space=pltpu.VMEM)] * len(out_shape),
        scratch_shapes=scratch_shapes,
        compiler_params=pltpu.CompilerParams(collective_id=collective_id, has_side_effects=True),
    )(*operands)


def decode(encoded, kv_all, span_queries, span_count):
    dec_kv = jnp.einsum(
        "re,nsec->rsnc", encoded.reshape(-1, E), kv_all, preferred_element_type=jnp.float32
    ).astype(jnp.bfloat16)
    head_count = span_queries.shape[1] // HD
    dec_kv = dec_kv.reshape(NB, span_count, PT, 2, head_count, HD)
    dec_query = span_queries.reshape(span_count, CT, head_count, HD)
    scores = jnp.einsum(
        "cqhd,ncphd->chqnp", dec_query, dec_kv[:, :, :, 0], preferred_element_type=jnp.float32
    ) / math.sqrt(HD)
    scores = scores.reshape(span_count, head_count, CT, NB * PT)
    weights = softmax_rows(scores).astype(jnp.bfloat16)
    weights = weights.reshape(span_count, head_count, CT, NB, PT)
    attended = jnp.einsum(
        "chqnp,ncphd->cqhd", weights, dec_kv[:, :, :, 1], preferred_element_type=jnp.float32
    )
    return attended.astype(jnp.bfloat16).reshape(span_count * CT, head_count * HD)


def body(
    span_states,
    span_queries,
    span_memory,
    passages,
    neighbours,
    enc_query_w,
    enc_out_w,
    kv_weight,
    out_weight,
):
    n = lax.axis_size("span")
    span_count = neighbours.shape[0]
    bf16 = jnp.bfloat16
    dma = pltpu.SemaphoreType.DMA
    half_rows = PT // 2
    kv = kv_weight.transpose(1, 0, 2)
    memory = span_memory.transpose(1, 2, 0)
    rows, tokens = span_count * PT, span_memory.shape[0]
    sds = jax.ShapeDtypeStruct
    fused = kv.shape[2] % HD == 0
    enc_shape, kv_shape = (NB, rows, E), (n,) + kv.shape
    states, width = sds(span_states.shape, bf16), out_weight.shape[1]
    out_scratch = [
        pltpu.VMEM((n,) + span_queries.shape, bf16),
        pltpu.VMEM((n, 2, tokens // 2, width), bf16),
        pltpu.VMEM((n, tokens // 2, width), bf16),
        pltpu.VMEM((n, tokens // 2, width), bf16),
        pltpu.VMEM((n // 2, 2, tokens // 2, width), bf16),
        dma((2, 2, n // 2, 2)),
        dma((2, n)),
        dma((n,)),
        dma((n // 2, 2)),
    ]
    scratch = [
        pltpu.VMEM((passages.shape[0] // PT, 2, half_rows, E), bf16),
        pltpu.VMEM(span_queries.shape if fused else (16, 128), bf16),
        pltpu.VMEM((8, 128), jnp.int32),
        pltpu.VMEM((n, 8, 128), jnp.int32),
        pltpu.SMEM((n, 8, 128), jnp.int32),
        pltpu.VMEM((n, half_rows, E), bf16),
        pltpu.VMEM((n, half_rows, E), bf16),
        pltpu.VMEM((span_count, half_rows, E), bf16),
        pltpu.VMEM((rows, E), bf16),
        pltpu.VMEM((2, E, tokens), bf16),
        pltpu.VMEM((E, E), bf16),
        pltpu.VMEM((E, E), bf16),
        pltpu.VMEM((rows, E), bf16),
        pltpu.VMEM((rows, E), bf16),
        dma((11,)),
        dma((2, n)),
        dma((2, n)),
        dma((2, span_count)),
        dma((2, 4)),
        dma((2,)),
        dma((2, 2, n // 2, 4)),
        dma((2, 2, n // 2, 2)),
    ]
    if fused:
        scratch = [
            pltpu.VMEM(enc_shape, bf16), pltpu.VMEM(kv_shape, bf16), pltpu.VMEM(span_queries.shape, bf16),
            pltpu.VMEM(out_weight.shape, bf16), pltpu.VMEM(span_states.shape, bf16),
        ] + out_scratch + scratch
    found = call(
        functools.partial(fetch_kernel, n, lax.axis_size("groups"), span_count, fused), 0,
        [states] if fused else [sds(enc_shape, bf16), sds(kv_shape, bf16)],
        scratch, [pltpu.VMEM] + [pl.ANY] * 8,
        neighbours, passages.reshape(-1, 2, half_rows, E), memory, enc_query_w.T, enc_out_w.T, kv,
        span_queries, out_weight, span_states,
    )
    if fused:
        return found[0]
    attended = decode(found[0], found[1], span_queries, span_count)
    return call(
        functools.partial(out_kernel, n), 1, [states], out_scratch, [pltpu.VMEM] * 3,
        attended, out_weight, span_states,
    )[0]


def solution(mesh):
    placed = (
        P(("groups", "span"), "head"),
        P(("groups", "span"), "head"),
        P(("groups", "span"), None, "head"),
        P(("groups", "span"), None),
        P(("groups", "span"), None),
        P(None, "head"),
        P(None, "head"),
        P(None, None, ("head", "span")),
        P("head", "span"),
    )
    return jax.shard_map(
        body, mesh=mesh, in_specs=placed, out_specs=P(("groups", "span"), "head"), check_vma=False
    )
```

```python
import functools
import math

import jax
import jax.numpy as jnp
from jax import lax
from jax.experimental import pallas as pl
from jax.experimental.pallas import tpu as pltpu
from jax.sharding import PartitionSpec as P

HD = 128
E = 896
EHD = 64
CT = 64
PT = 128
NB = 2
PS_DEV = 8
MESH = pl.DeviceIdType.MESH


epsilon = 1e-06


def rms_rows(values):
    return values * lax.rsqrt(jnp.mean(values * values, axis=-1, keepdims=True) + epsilon)


def softmax_rows(scores):
    top_score = jnp.max(scores, axis=-1, keepdims=True)
    raised = jnp.exp(scores - top_score)
    return raised / jnp.sum(raised, axis=-1, keepdims=True)


def ring_place(span, n):
    odd = span % 2
    return (1 - odd) * (span // 2) + odd * (n - 1 - span // 2)


def ring_span(place, n):
    back = place // (n // 2)
    return (1 - back) * (2 * place) + back * (2 * (n - 1 - place) + 1)


def remote(src, dst, send_sem, recv_sem, **where):
    return pltpu.make_async_remote_copy(
        src_ref=src, dst_ref=dst, send_sem=send_sem, recv_sem=recv_sem,
        device_id=where, device_id_type=MESH,
    )


class Ring:
    def __init__(self, n, own, slots, sems):
        me = lax.axis_index("span")
        self.n, self.own, self.slots, self.sems = n, own, slots, sems
        self.place = ring_place(me, n)
        self.targets = (ring_span((self.place + 1) % n, n), ring_span((self.place + n - 1) % n, n))
        self.steps = n // 2
        self.copies = {}

    def travels(self, t, side, k):
        return t < self.steps - 1 or k % 2 == side

    def block(self, t, side):
        n = self.n
        return ring_span((self.place + (n - t if side == 0 else t)) % n, n)

    def send(self, t, side, k):
        dst = self.slots(self.block(t, side))[k]
        copy = remote(
            self.own[k] if t == 0 else dst, dst,
            self.sems.at[0, side, t, k], self.sems.at[1, side, t, k], span=self.targets[side],
        )
        copy.start()
        self.copies[t, side, k] = copy

    def start(self):
        for k in range(len(self.own)):
            for side in range(2):
                if self.travels(0, side, k):
                    self.send(0, side, k)

    def advance(self, t, forward=None):
        for k in range(len(self.own)):
            for side in range(2):
                if self.travels(t, side, k):
                    self.copies[t, side, k].wait_recv()
                    if t + 1 < self.steps and self.travels(t + 1, side, k):
                        self.send(t + 1, side, k)
                    if forward is not None:
                        forward(t, side, k, self.block(t + 1, side))
        return [self.block(t + 1, side) for side in range(1 if t == self.steps - 1 else 2)]

    def finish(self):
        for copy in self.copies.values():
            copy.wait_send()


def weigh(scores, mask):
    scores = jnp.where(mask, scores, -jnp.inf)
    raised = jnp.exp(scores - jnp.max(scores, axis=-1, keepdims=True))
    return (raised * (1.0 / jnp.sum(raised, axis=-1, keepdims=True))).astype(jnp.bfloat16)


def same_span(shape, rows_each, lanes_each, spans):
    row = lax.broadcasted_iota(jnp.int32, shape, 0) // rows_each
    lane = (lax.broadcasted_iota(jnp.int32, shape, 1) // lanes_each) % spans
    return row == lane


def dot(a, b, dims=((1,), (0,))):
    return lax.dot_general(a, b, (dims, ((), ())), preferred_element_type=jnp.float32)


def greet_all(n):
    me = lax.axis_index("span")
    head = lax.axis_index("head")
    barrier = pltpu.get_barrier_semaphore()
    for d in range(n):
        for hop in range(2):
            if d or hop:
                pl.semaphore_signal(
                    barrier, inc=1,
                    device_id={"span": (me + d) % n, "head": (head + hop) % 2}, device_id_type=MESH,
                )
    return barrier, 2 * n - 1


def fetch_kernel(
    n, groups, spans, fused, nb_ref, pas_in, mem_ref, wq_ref, wo_ref, kv_ref, ask_in, w_in, states_in, *rest,
):
    if fused:
        (out_ref, enc, kvg, att_ref, *tail) = rest[:4 + 11]
        scratch = rest[4 + 11:]
    else:
        enc, kvg = rest[:2]
        scratch = rest[2:]
    (
        pas_ref, ask_ref, nb_own, nbg, nbs, picks, got, swap, cop, mem, wq, wo, query, mixed,
        local_sem, nb_sem, pas_sem, swap_sem, w_sem, enc_sem, ring_sem, twin_sem,
    ) = scratch
    me = lax.axis_index("span")
    head = lax.axis_index("head")
    group = lax.axis_index("groups")
    other = 1 - head
    twin = group + 1 - 2 * (group % 2)
    part = group % 2
    half_rows = PT // 2
    half_e = wq_ref.shape[0]
    barrier, greeted = greet_all(n)
    pl.semaphore_signal(barrier, inc=1, device_id={"groups": twin}, device_id_type=MESH)
    loads = [pltpu.make_async_copy(pas_in, pas_ref, local_sem.at[7])]
    if fused:
        loads += [
            pltpu.make_async_copy(ask_in, ask_ref, local_sem.at[8]),
            pltpu.make_async_copy(w_in, tail[0], local_sem.at[9]),
            pltpu.make_async_copy(states_in, tail[1], local_sem.at[10]),
        ]
    for copy in loads:
        copy.start()
    nb_own[...] = jnp.zeros_like(nb_own)
    nb_own[:spans, :NB] = nb_ref[...]
    pl.semaphore_wait(barrier, greeted + 1)

    nb_copies = []
    for d in range(1, n):
        copy = remote(nb_own, nbg.at[me], nb_sem.at[0, d], nb_sem.at[1, d], span=(me + d) % n)
        copy.start()
        nb_copies.append(copy)
    own_nb = pltpu.make_async_copy(nb_own, nbg.at[me], local_sem.at[0])
    own_nb.start()

    depth = kv_ref.shape[1]
    half, extra = depth // 2, depth // 28 * 3
    near, far = part, 1 - part

    def pieces(ref):
        return [
            ref.at[near, pl.ds(0, half)], ref.at[near, pl.ds(half, half)],
            ref.at[far, pl.ds(0, extra // 2)], ref.at[far, pl.ds(extra // 2, extra // 2)],
        ]

    ring = Ring(n, pieces(kv_ref), lambda block: pieces(kvg.at[block]), ring_sem)
    twins = [[] for _ in range(ring.steps)]

    def to_twin(t, side, k, block):
        if k < 2:
            lines = pl.ds(extra, half - extra) if k == 0 else pl.ds(half, half)
            piece = kvg.at[block, near, lines]
            copy = remote(piece, piece, twin_sem.at[0, side, t, k], twin_sem.at[1, side, t, k], groups=twin)
            copy.start()
            twins[t].append(copy)

    ring.start()
    mine = pl.ds(pl.multiple_of(head * half_e, half_e), half_e)
    w_copies, own_copies = [], []
    for i, (src, dst) in enumerate((
        (mem_ref.at[0], mem.at[0, mine]), (mem_ref.at[1], mem.at[1, mine]), (wq_ref, wq.at[mine]), (wo_ref, wo.at[mine]),
    )):
        w_copies.append(remote(src, dst, w_sem.at[0, i], w_sem.at[1, i], head=other))
        w_copies[-1].start()
        own_copies.append(pltpu.make_async_copy(src, dst, local_sem.at[3 + i]))
        own_copies[-1].start()
    own_copies.append(pltpu.make_async_copy(kv_ref, kvg.at[me], local_sem.at[1]))
    own_copies[-1].start()
    own_nb.wait()
    loads[0].wait()
    for copy in nb_copies:
        copy.wait()
    to_scalar = pltpu.make_async_copy(nbg, nbs, local_sem.at[2])
    to_scalar.start()
    to_scalar.wait()

    def pick(requester):
        index = jnp.int32(0)
        for e in range(spans * NB):
            wanted = nbs[requester, e // NB, e % NB]
            index = index + jnp.where(wanted // PS_DEV == me, wanted % PS_DEV, 0)
        return pas_ref[index, head]

    pas_copies = []
    picks[1] = pick((me + 1) % n)
    for d in range(1, n):
        if d + 1 < n:
            picks[d + 1] = pick((me + d + 1) % n)
        else:
            got[me] = pick(me)
        copy = remote(picks.at[d], got.at[me], pas_sem.at[0, d], pas_sem.at[1, d], span=(me + d) % n)
        copy.start()
        pas_copies.append(copy)

    arrivals = [ring.advance(0, to_twin)]
    for copy in pas_copies:
        copy.wait_recv()
    swaps = []
    for c in range(spans):
        swap[c] = got[nbs[me, c, other] // PS_DEV]
    for c in range(spans):
        spot = cop.at[pl.ds(pl.multiple_of(c * PT + head * half_rows, half_rows), half_rows)]
        copy = remote(swap.at[c], spot, swap_sem.at[0, c], swap_sem.at[1, c], head=other)
        copy.start()
        swaps.append(copy)
        spot[...] = got[nbs[me, c, head] // PS_DEV]
    for copy in own_copies:
        copy.wait()
    for copy in w_copies:
        copy.wait()
    for copy in swaps:
        copy.wait()

    arrivals.append(ring.advance(1, to_twin))
    rows = cop.shape[0]
    tokens = mem.shape[2]
    width = cop.shape[1]
    values = cop[...].astype(jnp.float32)
    query[...] = dot(rms_rows(values).astype(jnp.bfloat16), wq[...], ((1,), (1,))).astype(jnp.bfloat16)
    mask = same_span((rows, tokens), PT, CT, spans)
    feature = lax.broadcasted_iota(jnp.int32, (2 * EHD, tokens), 0) // EHD
    for j in range(width // (2 * EHD)):
        lines = pl.ds(j * 2 * EHD, 2 * EHD)
        total = None
        for e in range(2):
            keys = jnp.where(feature == e, mem[0, lines], jnp.bfloat16(0))
            vals = jnp.where(feature == e, mem[1, lines], jnp.bfloat16(0))
            scores = dot(query[:, lines], keys) * (1.0 / math.sqrt(EHD))
            term = dot(weigh(scores, mask), vals, ((1,), (1,)))
            total = term if e == 0 else total + term
        mixed[:, lines] = total.astype(jnp.bfloat16)
    branch = dot(mixed[...], wo[...])
    enc[head] = rms_rows(cop[...].astype(jnp.float32) + branch).astype(jnp.bfloat16)
    enc_copy = remote(enc.at[head], enc.at[head], enc_sem.at[0], enc_sem.at[1], head=other)
    enc_copy.start()
    if ring.steps > 2:
        arrivals.append(ring.advance(2, to_twin))
    enc_copy.wait_recv()

    if fused:
        loads[1].wait()
        asks = ask_ref.shape[0]
        dec_mask = same_span((asks, NB * rows), CT, PT, spans)

        def attend(block):
            for m in range(kv_ref.shape[2] // HD):
                flat = enc[...].reshape(NB * rows, width)
                lanes = pl.ds(m * HD, HD)
                keys = dot(flat, kvg[block, 0, :, lanes]).astype(jnp.bfloat16)
                vals = dot(flat, kvg[block, 1, :, lanes]).astype(jnp.bfloat16)
                spot = pl.ds(pl.multiple_of(block * kv_ref.shape[2] + m * HD, HD), HD)
                scores = dot(ask_ref[:, spot], keys, ((1,), (1,))) * (1.0 / math.sqrt(HD))
                att_ref[:, spot] = dot(weigh(scores, dec_mask), vals).astype(jnp.bfloat16)

        attend(me)

    for t in range(ring.steps):
        while len(arrivals) < min(t + 3, ring.steps):
            arrivals.append(ring.advance(len(arrivals), to_twin))
        for copy in twins[t]:
            copy.wait_recv()
        if fused:
            for block in arrivals[t]:
                attend(block)
    if fused:
        loads[2].wait()
        loads[3].wait()
        out_stage(n, att_ref, tail[0], tail[1], out_ref, *tail[2:])
    enc_copy.wait_send()
    for copy in pas_copies + [copy for pair in twins for copy in pair]:
        copy.wait_send()
    ring.finish()


def out_kernel(n, *refs):
    barrier, greeted = greet_all(n)
    pl.semaphore_wait(barrier, greeted)
    out_stage(n, *refs)


def out_stage(
    n, att_ref, w_ref, states_ref, out_ref,
    gathered, part, crossed, summed, back, ring_sem, cross_sem, send_sem, back_sem,
):
    me = lax.axis_index("span")
    head = lax.axis_index("head")
    other = 1 - head
    half = n // 2
    owner_head = me // half
    column = me % half
    rows = att_ref.shape[0]
    half_rows = rows // 2
    width = w_ref.shape[1]

    def pieces(ref):
        return [ref.at[pl.ds(k * half_rows, half_rows)] for k in range(2)]

    ring = Ring(n, pieces(att_ref), lambda block: pieces(gathered.at[block]), ring_sem)
    ring.start()
    crossings, returns = [], []

    def project(block, rows_ref):
        i = len(crossings)
        value = jnp.dot(rows_ref[...], w_ref[...], preferred_element_type=jnp.float32)
        value = value.astype(jnp.bfloat16)
        part[i, 0] = value[:half_rows]
        part[i, 1] = value[half_rows:]
        copy = remote(part.at[i, other], crossed.at[i], cross_sem.at[0, i], cross_sem.at[1, i], head=other)
        crossings.append((copy, block))

    def send_across():
        crossings[-1][0].start()

    def give_back():
        i = len(returns)
        copy, block = crossings[i]
        copy.wait_recv()
        total = part[i, head].astype(jnp.float32) + crossed[i].astype(jnp.float32)
        summed[i] = total.astype(jnp.bfloat16)
        copy = remote(
            summed.at[i], back.at[column, head], send_sem.at[i], back_sem.at[column, head],
            span=block, head=owner_head,
        )
        if i == 0:
            @pl.when(head != owner_head)
            def _():
                copy.start()

            @pl.when(head == owner_head)
            def _():
                back[column, head] = summed[i]
        else:
            copy.start()
        returns.append(copy)

    project(me, att_ref)
    send_across()
    for t in range(ring.steps):
        for block in ring.advance(t):
            project(block, gathered.at[block])
            send_across()
            give_back()
    give_back()

    for j in range(half):
        for source in range(2):
            mine = (head * half + j == me) & (head == source)

            @pl.when(jnp.logical_not(mine))
            def _():
                remote(
                    summed.at[0], back.at[j, source], send_sem.at[0], back_sem.at[j, source], head=other,
                ).wait_recv()

            lanes = pl.ds(j * width, width)
            lines = pl.ds(source * half_rows, half_rows)
            out_ref[lines, lanes] = (
                states_ref[lines, lanes].astype(jnp.float32) + back[j, source].astype(jnp.float32)
            ).astype(jnp.bfloat16)
    ring.finish()
    for copy, _ in crossings:
        copy.wait_send()
    for i, copy in enumerate(returns):
        if i == 0:
            @pl.when(head != owner_head)
            def _():
                copy.wait_send()
        else:
            copy.wait_send()


def call(kernel, collective_id, out_shape, scratch_shapes, spaces, *operands):
    return pl.pallas_call(
        kernel,
        out_shape=out_shape,
        in_specs=[pl.BlockSpec(memory_space=space) for space in spaces],
        out_specs=[pl.BlockSpec(memory_space=pltpu.VMEM)] * len(out_shape),
        scratch_shapes=scratch_shapes,
        compiler_params=pltpu.CompilerParams(collective_id=collective_id, has_side_effects=True),
    )(*operands)


def decode(encoded, kv_all, span_queries, span_count):
    dec_kv = jnp.einsum(
        "re,nsec->rsnc", encoded.reshape(-1, E), kv_all, preferred_element_type=jnp.float32
    ).astype(jnp.bfloat16)
    head_count = span_queries.shape[1] // HD
    dec_kv = dec_kv.reshape(NB, span_count, PT, 2, head_count, HD)
    dec_query = span_queries.reshape(span_count, CT, head_count, HD)
    scores = jnp.einsum(
        "cqhd,ncphd->chqnp", dec_query, dec_kv[:, :, :, 0], preferred_element_type=jnp.float32
    ) / math.sqrt(HD)
    scores = scores.reshape(span_count, head_count, CT, NB * PT)
    weights = softmax_rows(scores).astype(jnp.bfloat16)
    weights = weights.reshape(span_count, head_count, CT, NB, PT)
    attended = jnp.einsum(
        "chqnp,ncphd->cqhd", weights, dec_kv[:, :, :, 1], preferred_element_type=jnp.float32
    )
    return attended.astype(jnp.bfloat16).reshape(span_count * CT, head_count * HD)


def body(
    span_states,
    span_queries,
    span_memory,
    passages,
    neighbours,
    enc_query_w,
    enc_out_w,
    kv_weight,
    out_weight,
):
    n = lax.axis_size("span")
    span_count = neighbours.shape[0]
    bf16 = jnp.bfloat16
    dma = pltpu.SemaphoreType.DMA
    half_rows = PT // 2
    kv = kv_weight.transpose(1, 0, 2)
    memory = span_memory.transpose(1, 2, 0)
    rows, tokens = span_count * PT, span_memory.shape[0]
    sds = jax.ShapeDtypeStruct
    fused = kv.shape[2] % HD == 0
    enc_shape, kv_shape = (NB, rows, E), (n,) + kv.shape
    states, width = sds(span_states.shape, bf16), out_weight.shape[1]
    out_scratch = [
        pltpu.VMEM((n,) + span_queries.shape, bf16),
        pltpu.VMEM((n, 2, tokens // 2, width), bf16),
        pltpu.VMEM((n, tokens // 2, width), bf16),
        pltpu.VMEM((n, tokens // 2, width), bf16),
        pltpu.VMEM((n // 2, 2, tokens // 2, width), bf16),
        dma((2, 2, n // 2, 2)),
        dma((2, n)),
        dma((n,)),
        dma((n // 2, 2)),
    ]
    scratch = [
        pltpu.VMEM((passages.shape[0] // PT, 2, half_rows, E), bf16),
        pltpu.VMEM(span_queries.shape if fused else (16, 128), bf16),
        pltpu.VMEM((8, 128), jnp.int32),
        pltpu.VMEM((n, 8, 128), jnp.int32),
        pltpu.SMEM((n, 8, 128), jnp.int32),
        pltpu.VMEM((n, half_rows, E), bf16),
        pltpu.VMEM((n, half_rows, E), bf16),
        pltpu.VMEM((span_count, half_rows, E), bf16),
        pltpu.VMEM((rows, E), bf16),
        pltpu.VMEM((2, E, tokens), bf16),
        pltpu.VMEM((E, E), bf16),
        pltpu.VMEM((E, E), bf16),
        pltpu.VMEM((rows, E), bf16),
        pltpu.VMEM((rows, E), bf16),
        dma((11,)),
        dma((2, n)),
        dma((2, n)),
        dma((2, span_count)),
        dma((2, 4)),
        dma((2,)),
        dma((2, 2, n // 2, 4)),
        dma((2, 2, n // 2, 2)),
    ]
    if fused:
        scratch = [
            pltpu.VMEM(enc_shape, bf16), pltpu.VMEM(kv_shape, bf16), pltpu.VMEM(span_queries.shape, bf16),
            pltpu.VMEM(out_weight.shape, bf16), pltpu.VMEM(span_states.shape, bf16),
        ] + out_scratch + scratch
    found = call(
        functools.partial(fetch_kernel, n, lax.axis_size("groups"), span_count, fused), 0,
        [states] if fused else [sds(enc_shape, bf16), sds(kv_shape, bf16)],
        scratch, [pltpu.VMEM] + [pl.ANY] * 8,
        neighbours, passages.reshape(-1, 2, half_rows, E), memory, enc_query_w.T, enc_out_w.T, kv,
        span_queries, out_weight, span_states,
    )
    if fused:
        return found[0]
    attended = decode(found[0], found[1], span_queries, span_count)
    return call(
        functools.partial(out_kernel, n), 1, [states], out_scratch, [pltpu.VMEM] * 3,
        attended, out_weight, span_states,
    )[0]


def solution(mesh):
    placed = (
        P(("groups", "span"), "head"),
        P(("groups", "span"), "head"),
        P(("groups", "span"), None, "head"),
        P(("groups", "span"), None),
        P(("groups", "span"), None),
        P(None, "head"),
        P(None, "head"),
        P(None, None, ("head", "span")),
        P("head", "span"),
    )
    return jax.shard_map(
        body, mesh=mesh, in_specs=placed, out_specs=P(("groups", "span"), "head"), check_vma=False
    )
```
